32 devices in a mesh: section: 4 (over y, x), dp: 8 (over z, core).
Axes of the slice: x: 2, y: 2, z: 4, core: 2. Of those that a mesh axis runs over, the one named last changes fastest.
Arguments:
- momentum: float32 [4, 4, 3584, 288], P('section', None, 'dp'), may hold values from -6 to 6
- gradient: bfloat16 [4, 4, 3584, 288], P('section', None, 'dp'), may hold values from -1300 to 1300
- assignment: int32 [4, 4], P('section'), may hold values from 0 to 7, as said below
Outputs:
- new_momentum: float32 [4, 4, 3584, 288], P('section', None, 'dp')
- update: bfloat16 [4, 4, 3584, 288], P('section', None, 'dp')
- slot_rms: float32 [4, 16], P('section', 'dp')
The draws below stay inside these ranges and needn't reach their ends.
Inputs may be any that keep to these rules, and one draw needn't show every extreme that they name: `assignment`: within one section no owner holds more than 2 matrices, and some owner holds exactly 2.
All inputs are finite; a program needn't handle non-finite values.
Results may differ from the reference program's by a relative error of at most 0.015.
The reference program's roundings to bfloat16 on the way count: a program that leaves them out, or rounds other values in their place, can miss the bound.
Values may be sent and summed in bfloat16 or wider, within the bound.
No kernel may reach another device: no remote copies, remote signals or barrier semaphores. Data moves between devices by JAX's collectives and lax.ppermute only.
A program may use at most 64 MiB of HBM per device.

```python
import math
import jax
import jax.numpy as jnp
from jax import lax

D_IN = 3584
KV = 288
MAXOWN = 2
NS_STEPS = 5
LAYERS = 4
N_SECTION = 4
N_DP = 8


def draw_gradient(key, part):
    full_shape = (N_SECTION, LAYERS, D_IN, KV)
    position = (jnp.arange(N_SECTION, dtype=jnp.float32)[:, None] * D_IN + jnp.arange(D_IN, dtype=jnp.float32)[None, :]) / (N_SECTION * D_IN)
    column = jnp.arange(KV, dtype=jnp.float32) / KV
    first_key = jax.random.fold_in(key, 11)
    row_scale = 10.0 ** position
    col_scale = 10.0 ** column
    mixed_core = jax.random.truncated_normal(first_key, -4.0, 4.0, full_shape, jnp.float32)
    values = mixed_core * row_scale[:, None, :, None] * col_scale[None, None, None, :]
    return values.astype(jnp.bfloat16)


def draw_assignment(key, part):
    doubled = LAYERS // 4
    single = LAYERS - doubled
    rows_out = []
    for section_index in range(N_SECTION):
        section_key = jax.random.fold_in(key, 101 + section_index)
        chosen = jax.random.permutation(section_key, N_DP)
        owner_list = jnp.concatenate([chosen[:single], chosen[:doubled]])
        shuffle = jax.random.permutation(jax.random.fold_in(section_key, 7), LAYERS)
        rows_out.append(owner_list[shuffle])
    return jnp.stack(rows_out).astype(jnp.int32)


def block_levels(own_key, shape, split, smallest, top_value):
    level, own = 1.0, jax.random.fold_in(own_key, 6)
    for axis_at, shards_of in split:
        steps = jnp.exp(jax.random.uniform(jax.random.fold_in(own, axis_at), (shards_of,), jnp.float32, smallest / len(split), top_value / len(split)))
        level = level * jnp.repeat(steps, shape[axis_at] // shards_of).reshape([-1 if axis == axis_at else 1 for axis in range(len(shape))])
    return level


def centred(own_key, shape, spread, limit, shards=(), kind=jnp.bfloat16):
    loudness = block_levels(own_key, shape, shards, -0.22, 0.18) if shards else 1.0
    array = jax.random.normal(own_key, shape, jnp.float32) * spread * loudness
    return jnp.minimum(jnp.maximum(array, -limit), limit).astype(kind)


def setup_inputs(seed: int = 0) -> dict:
    key_list = jax.random.split(jax.random.key(seed), 4)
    return {
        "momentum": centred(key_list[0], (N_SECTION, LAYERS, D_IN, KV), 1.0, 6.0, ((0, 4), (2, 8)), jnp.float32),
        "gradient": draw_gradient(jax.random.fold_in(key_list[3], 71), 0),
        "assignment": draw_assignment(jax.random.fold_in(key_list[3], 71), 0),
    }


momentum_decay = 0.95
clip_rms = 0.5
newton_coeffs = (3.4445, -4.775, 2.0315)

def newton(matrix):
    values = matrix.astype(jnp.float32)
    squares = jnp.sum(values * values)
    current = (values / (jnp.sqrt(squares) + 1e-07)).astype(jnp.bfloat16)
    for iteration in range(NS_STEPS):
        gram_mat = jnp.dot(current.T, current, preferred_element_type=jnp.float32).astype(jnp.bfloat16)
        square_mat = jnp.dot(gram_mat, gram_mat, preferred_element_type=jnp.float32)
        mixing = (newton_coeffs[1] * gram_mat.astype(jnp.float32) + newton_coeffs[2] * square_mat).astype(jnp.bfloat16)
        following = newton_coeffs[0] * current.astype(jnp.float32) + jnp.dot(current, mixing, preferred_element_type=jnp.float32)
        if iteration == NS_STEPS - 1:
            following = following * math.sqrt(D_IN)
        current = following.astype(jnp.bfloat16)
    return current

def reference(momentum, gradient, assignment):
    grads = gradient.astype(jnp.float32)
    total_sq = jnp.sum(grads * grads)
    entries = grads.size
    factor = clip_rms / jnp.sqrt(total_sq / entries + 1e-06)
    fresh = momentum_decay * momentum + factor * grads
    nesterov = (factor * grads + momentum_decay * fresh).astype(jnp.bfloat16)
    flat = nesterov.reshape(N_SECTION * LAYERS, D_IN, KV)
    ortho = lax.map(newton, flat)
    ortho32 = ortho.astype(jnp.float32)
    mean_sq = (lax.optimization_barrier(jnp.sum(ortho32 * ortho32, axis=(1, 2))) / (D_IN * KV)).reshape(N_SECTION, LAYERS)
    positions = jnp.arange(LAYERS, dtype=jnp.int32)
    shared = assignment[:, :, None] == assignment[:, None, :]
    earlier = positions[None, None, :] < positions[None, :, None]
    slot_index = lax.optimization_barrier(jnp.sum((shared & earlier).astype(jnp.int32), axis=2)).astype(jnp.int32)
    target = (assignment * MAXOWN + slot_index).astype(jnp.int32)
    placing = (jnp.arange(N_DP * MAXOWN, dtype=jnp.int32)[None, :, None] == target[:, None, :]).astype(jnp.float32)
    slot_rms = lax.optimization_barrier(jnp.sum(placing * mean_sq[:, None, :], axis=2))
    return (fresh, ortho.reshape(N_SECTION, LAYERS, D_IN, KV), slot_rms)
```

```python
import functools
import math

import jax
import jax.numpy as jnp
from jax import lax
from jax.experimental import pallas as pl
from jax.experimental.pallas import tpu as pltpu
from jax.sharding import PartitionSpec as P

MAXOWN = 2
NS_STEPS = 5
LANES = 128

momentum_decay = 0.95
clip_rms = 0.5
newton_coeffs = (3.4445, -4.775, 2.0315)

F32 = jnp.float32
BF16 = jnp.bfloat16


def whole(shape):
    return pl.BlockSpec(shape, lambda *_: (0,) * len(shape))


def total_of(values):
    return jnp.sum(jnp.sum(values, axis=0, keepdims=True), axis=1, keepdims=True)


def sums_kernel(grad_ref, mom_ref, out_ref):
    layer = pl.program_id(0)

    @pl.when(layer == 0)
    def _():
        out_ref[...] = jnp.zeros_like(out_ref)

    grads = grad_ref[0].astype(F32)
    moms = mom_ref[0]
    gg, gm, mm = total_of(grads * grads), total_of(grads * moms), total_of(moms * moms)
    lane = lax.broadcasted_iota(jnp.int32, (1, out_ref.shape[1]), 1)
    first = 1 + 3 * layer
    row = jnp.where((lane == 0) | (lane == first), gg, 0.0)
    row = row + jnp.where(lane == first + 1, gm, 0.0) + jnp.where(lane == first + 2, mm, 0.0)
    out_ref[...] += jnp.broadcast_to(row, out_ref.shape)


def block_rows(width):
    tail = width - 2 * LANES
    return 3 * LANES + 3 * tail


def start_kernel(
    entries, owners, scal_ref, sums_ref, grad_ref, mom_ref, start_ref, keep_ref, send_ref, fac_ref, pack
):
    layer = pl.program_id(0)
    core, section = scal_ref[1], scal_ref[2]
    sums = sums_ref[...]
    lane = lax.broadcasted_iota(jnp.int32, sums.shape, 1)
    row = lax.broadcasted_iota(jnp.int32, sums.shape, 0)
    mine = (row >= section * owners) & (row < (section + 1) * owners)
    total = total_of(jnp.where(lane == 0, sums, 0.0))
    first = 1 + 3 * layer
    gg = total_of(jnp.where(mine & (lane == first), sums, 0.0))
    gm = total_of(jnp.where(mine & (lane == first + 1), sums, 0.0))
    mm = total_of(jnp.where(mine & (lane == first + 2), sums, 0.0))
    factor = clip_rms / jnp.sqrt(total / entries + 1e-06)
    fac_ref[...] = jnp.broadcast_to(factor, fac_ref.shape)
    on_grad = factor * (1.0 + momentum_decay)
    on_mom = momentum_decay * momentum_decay
    guess = on_grad * on_grad * gg + 2.0 * (on_grad * on_mom) * gm + (on_mom * on_mom) * mm
    guess = jnp.maximum(guess, 0.0)
    scale = 1.0 / (jnp.sqrt(guess) + 1e-07)
    scaled = factor * grad_ref[0].astype(F32)
    fresh = momentum_decay * mom_ref[0] + scaled
    nesterov = (scaled + momentum_decay * fresh).astype(BF16).astype(F32)
    squares = total_of(nesterov * nesterov)
    start = (nesterov * scale).astype(BF16)
    start_ref[0] = start
    gram = lax.dot_general(start, start, (((1,), (1,)), ((), ())), preferred_element_type=F32)
    width = start.shape[0]
    tail = width - 2 * LANES
    a, b = LANES, 2 * LANES
    pack[0:a, :] = gram[0:a, 0:a]
    pack[a:b, :] = gram[0:a, a:b]
    pack[b : b + a, :] = gram[a:b, a:b]
    at = b + a
    pack[at : at + tail, :] = gram[b:, 0:a]
    pack[at + tail : at + 2 * tail, :] = gram[b:, a:b]
    spot = lax.broadcasted_iota(jnp.int32, (tail, LANES), 1)
    extra = jnp.where(spot == 64, squares, 0.0) + jnp.where(spot == 65, guess, 0.0)
    pack[at + 2 * tail :, :] = extra
    pack[at + 2 * tail :, 0:tail] = gram[b:, b:]
    half = pack.shape[0] // 2
    keep_ref[0] = pack[pl.ds(pl.multiple_of(core * half, 8), half), :]
    send_ref[0] = pack[pl.ds(pl.multiple_of((1 - core) * half, 8), half), :]


def split(value):
    high = value.astype(BF16)
    return high, (value - high.astype(F32)).astype(BF16)


def dot(left, right):
    return jnp.dot(left, right, preferred_element_type=F32)


def newton_kernel(owners, width, scal_ref, own_ref, other_ref, both_ref, mine_ref, pack):
    core = scal_ref[1]
    half = own_ref.shape[0]
    pack[pl.ds(pl.multiple_of(core * half, 8), half), :] = own_ref[...]
    pack[pl.ds(pl.multiple_of((1 - core) * half, 8), half), :] = other_ref[...]
    tail = width - 2 * LANES
    a, b = LANES, 2 * LANES
    at = b + a
    t00, t01, t11 = pack[0:a, :], pack[a:b, :], pack[b:at, :]
    t20, t21 = pack[at : at + tail, :], pack[at + tail : at + 2 * tail, :]
    last = pack[at + 2 * tail :, :]
    t22 = last[:, 0:tail]
    squares = last[0:1, 64:65]
    guess = last[0:1, 65:66] * (1.0 / owners)
    ratio = (jnp.sqrt(guess) + 1e-07) / (jnp.sqrt(squares) + 1e-07)
    gram = jnp.concatenate(
        [
            jnp.concatenate([t00, t01, t20.T], axis=1),
            jnp.concatenate([t01.T, t11, t21.T], axis=1),
            jnp.concatenate([t20, t21, t22], axis=1),
        ],
        axis=0,
    )
    gram = gram * (ratio * ratio)
    ca, cb, cc = newton_coeffs
    rows = lax.broadcasted_iota(jnp.int32, (width, width), 0)
    cols = lax.broadcasted_iota(jnp.int32, (width, width), 1)
    prod = None
    mean_sq = None
    for step in range(NS_STEPS):
        rounded = gram.astype(BF16)
        mix = (cb * rounded.astype(F32) + cc * dot(rounded, rounded)).astype(BF16)
        mix32 = mix.astype(F32)
        gram_hi, gram_lo = split(gram)
        if prod is None:
            prod = ratio * (jnp.where(rows == cols, ca, 0.0) + mix32)
            turned = ca * gram + dot(gram_hi, mix) + dot(gram_lo, mix)
        else:
            prod_hi, prod_lo = split(prod)
            turned = ca * gram + dot(gram_hi, mix) + dot(gram_lo, mix)
            prod = ca * prod + dot(prod_hi, mix) + dot(prod_lo, mix)
        if step < NS_STEPS - 1:
            turned_hi, turned_lo = split(turned)
            gram = ca * turned + dot(mix, turned_hi) + dot(mix, turned_lo)
        else:
            diagonal = jnp.where(rows == cols, turned, 0.0)
            mean_sq = total_of(ca * diagonal + mix32 * turned) * (1.0 / width)
    prod_hi, prod_lo = split(prod)
    mean_hi, mean_lo = split(jnp.broadcast_to(mean_sq, (width, LANES)))
    both_ref[0, :, 0:width] = prod_hi
    both_ref[1, :, 0:width] = prod_lo
    free = both_ref.shape[2] - width
    both_ref[0, :, width:] = mean_hi[:, 0:free]
    both_ref[1, :, width:] = mean_lo[:, 0:free]
    mine_ref[...] = both_ref[core]


def update_kernel(scale, width, chips, scal_ref, owner_ref, start_ref, high_ref, low_ref, out_ref, slot_ref):
    step = pl.program_id(0)
    layer = lax.rem(scal_ref[0] + step, chips)
    me = scal_ref[3]
    high, low = high_ref[0][:, 0:width], low_ref[0][:, 0:width]
    turn = (((0,), (0,)), ((), ()))
    start = start_ref[0]
    value = lax.dot_general(high, start, turn, preferred_element_type=F32)
    value = value + lax.dot_general(low, start, turn, preferred_element_type=F32)
    out_ref[0] = (value * scale).astype(BF16)
    mean_sq = high_ref[0][0:16, width:].astype(F32) + low_ref[0][0:16, width:].astype(F32)
    mean_sq = jnp.sum(jnp.where(
        (lax.broadcasted_iota(jnp.int32, mean_sq.shape, 0) == 0)
        & (lax.broadcasted_iota(jnp.int32, mean_sq.shape, 1) == 0), mean_sq, 0.0))

    @pl.when(step == 0)
    def _():
        for slot in range(MAXOWN):
            slot_ref[0, slot] = 0.0

    owner = owner_ref[0, layer]
    earlier = lax.fori_loop(
        0, layer, lambda i, n: n + jnp.where(owner_ref[0, i] == owner, 1, 0), jnp.int32(0)
    )
    for slot in range(MAXOWN):
        hit = (owner == me) & (earlier == slot)
        slot_ref[0, slot] = slot_ref[0, slot] + jnp.where(hit, mean_sq, 0.0)


def ring(size, by):
    return [(i, (i + 2 * by) % size) for i in range(size)]


def body(momentum, gradient, assignment):
    _, layers, rows, width = momentum.shape
    owners = lax.axis_size("dp")
    sections = lax.axis_size("section")
    chips = owners // 2
    assert chips == layers and width > 2 * LANES and width < 3 * LANES
    everyone = sections * owners
    entries = everyone * layers * rows * width
    mom = jnp.swapaxes(momentum[0], 1, 2)
    grad = jnp.swapaxes(gradient[0], 1, 2)
    place = lax.axis_index("dp")
    scal = jnp.stack([place // 2, place % 2, lax.axis_index("section"), place]).astype(jnp.int32)

    layer_spec = pl.BlockSpec((1, width, rows), lambda l, *_: (l, 0, 0))
    sum_width = -(-(1 + 3 * layers) // LANES) * LANES
    sums = pl.pallas_call(
        sums_kernel,
        grid=(layers,),
        in_specs=[layer_spec, layer_spec],
        out_specs=whole((everyone, sum_width)),
        out_shape=jax.ShapeDtypeStruct((everyone, sum_width), F32),
        name="sums",
    )(grad, mom)
    sums = lax.all_to_all(sums, ("section", "dp"), 0, 0, tiled=True)

    packed = block_rows(width)
    half = packed // 2
    rel_spec = pl.BlockSpec((1, half, LANES), lambda l, s: (lax.rem(l - s[0] + chips, chips), 0, 0))
    start, keep, send, factor = pl.pallas_call(
        functools.partial(start_kernel, entries, owners),
        grid_spec=pltpu.PrefetchScalarGridSpec(
            num_scalar_prefetch=1,
            grid=(layers,),
            in_specs=[whole((everyone, sum_width)), layer_spec, layer_spec],
            out_specs=[layer_spec, rel_spec, rel_spec, whole((8, LANES))],
            scratch_shapes=[pltpu.VMEM((packed, LANES), F32)],
        ),
        out_shape=[
            jax.ShapeDtypeStruct((layers, width, rows), BF16),
            jax.ShapeDtypeStruct((layers, half, LANES), F32),
            jax.ShapeDtypeStruct((layers, half, LANES), F32),
            jax.ShapeDtypeStruct((8, LANES), F32),
        ],
        name="start",
    )(scal, sums, grad, mom)
    fresh = momentum_decay * momentum + factor[0, 0] * gradient.astype(F32)

    swap = [(i, i ^ 1) for i in range(owners)]
    sums_up = keep + lax.ppermute(send, "dp", swap)
    far = chips // 2
    quarter = half // 2
    up, down = sums_up[far][:quarter], sums_up[far][quarter:]
    for step in range(1, far + 1):
        up = lax.ppermute(up, "dp", ring(owners, 1))
        down = lax.ppermute(down, "dp", ring(owners, -1))
        if step == 1 and far > 0:
            zero = jnp.zeros((quarter, LANES), F32)
            up = jnp.concatenate([up, zero], axis=0)
            down = jnp.concatenate([zero, down], axis=0)
        if step < far:
            up = up + sums_up[far - step]
            down = down + sums_up[chips - (far - step)]
    own = sums_up[0] + up + down
    other = lax.ppermute(own, "dp", swap)

    wide = 3 * LANES
    both, mine = pl.pallas_call(
        functools.partial(newton_kernel, owners, width),
        grid_spec=pltpu.PrefetchScalarGridSpec(
            num_scalar_prefetch=1,
            grid=(1,),
            in_specs=[whole((half, LANES)), whole((half, LANES))],
            out_specs=[whole((2, width, wide)), whole((width, wide))],
            scratch_shapes=[pltpu.VMEM((packed, LANES), F32)],
        ),
        out_shape=[
            jax.ShapeDtypeStruct((2, width, wide), BF16),
            jax.ShapeDtypeStruct((width, wide), BF16),
        ],
        name="newton",
    )(scal, own, other)

    cut = width // 2
    parts = {0: mine}
    from_down, from_up = mine, mine
    for step in range(1, far):
        from_down = lax.ppermute(from_down, "dp", ring(owners, 1))
        from_up = lax.ppermute(from_up, "dp", ring(owners, -1))
        parts[chips - step] = from_down
        parts[step] = from_up
    parts[far] = jnp.concatenate(
        [
            lax.ppermute(from_down[:cut], "dp", ring(owners, 1)),
            lax.ppermute(from_up[cut:], "dp", ring(owners, -1)),
        ],
        axis=0,
    )
    held = jnp.stack([parts[k] for k in range(1, chips)])
    swapped = lax.ppermute(held, "dp", swap)
    first = (scal[1] == 0)
    high = jnp.concatenate([both[0:1], jnp.where(first, held, swapped)], axis=0)
    low = jnp.concatenate([both[1:2], jnp.where(first, swapped, held)], axis=0)

    abs_spec = pl.BlockSpec((1, width, rows), lambda k, s, _: (lax.rem(k + s[0], chips), 0, 0))
    prod_spec = pl.BlockSpec((1, width, wide), lambda k, *_: (k, 0, 0))
    update, slots = pl.pallas_call(
        functools.partial(update_kernel, math.sqrt(owners * rows), width, chips),
        grid_spec=pltpu.PrefetchScalarGridSpec(
            num_scalar_prefetch=2,
            grid=(layers,),
            in_specs=[abs_spec, prod_spec, prod_spec],
            out_specs=[abs_spec, pl.BlockSpec((1, MAXOWN), lambda *_: (0, 0), memory_space=pltpu.SMEM)],
        ),
        out_shape=[
            jax.ShapeDtypeStruct((layers, width, rows), BF16),
            jax.ShapeDtypeStruct((1, MAXOWN), F32),
        ],
        name="update",
    )(scal, assignment, start, high, low)
    return (fresh, jnp.swapaxes(update, 1, 2)[None], slots)


def solution(mesh):
    in_specs = (P("section", None, "dp", None), P("section", None, "dp", None), P("section", None))
    out_specs = (P("section", None, "dp", None), P("section", None, "dp", None), P("section", "dp"))
    return jax.shard_map(body, mesh=mesh, in_specs=in_specs, out_specs=out_specs, check_vma=False)
```

```python
import functools
import math

import jax
import jax.numpy as jnp
from jax import lax
from jax.experimental import pallas as pl
from jax.experimental.pallas import tpu as pltpu
from jax.sharding import PartitionSpec as P


MAXOWN = 2
NS_STEPS = 5
LANES = 128

momentum_decay = 0.95
clip_rms = 0.5
newton_coeffs = (3.4445, -4.775, 2.0315)

F32 = jnp.float32
BF16 = jnp.bfloat16


VMEM_BYTES = 12 * 2**20


def params():
    return pltpu.CompilerParams(vmem_limit_bytes=VMEM_BYTES)


def cost(flops, bytes_accessed):
    return pl.CostEstimate(flops=flops, bytes_accessed=bytes_accessed, transcendentals=0)


def over(count, visit):
    if count <= 8:
        for i in range(count):
            visit(i)
    else:
        pl.loop(0, count)(visit)


def whole(shape):
    return pl.BlockSpec(shape, lambda *_: (0,) * len(shape))


def total_of(values):
    return jnp.sum(jnp.sum(values, axis=0, keepdims=True), axis=1, keepdims=True)


def sums_kernel(layers, grad_in, mom_in, out_ref, grad_ref, mom_ref, acc, sems):
    def copies(layer):
        return (
            pltpu.make_async_copy(grad_in.at[layer], grad_ref.at[layer], sems.at[layer, 0]),
            pltpu.make_async_copy(mom_in.at[layer], mom_ref.at[layer], sems.at[layer, 1]),
        )

    def begin(layer):
        for copy in copies(layer):
            copy.start()

    def visit(layer):
        for copy in copies(layer):
            copy.wait()
        grads = grad_ref[layer].astype(F32)
        moms = mom_ref[layer]
        for i, prod in enumerate((grads * grads, grads * moms, moms * moms)):
            acc[pl.ds(3 * layer + i, 1), :] = jnp.sum(prod, axis=0, keepdims=True)

    acc[...] = jnp.zeros_like(acc)
    over(layers, begin)
    over(layers, visit)
    column = jnp.sum(acc[...], axis=1, keepdims=True)
    shape = (acc.shape[0], out_ref.shape[1])
    hit = lax.broadcasted_iota(jnp.int32, shape, 0) == lax.broadcasted_iota(jnp.int32, shape, 1)
    line = jnp.sum(jnp.where(hit, column, 0.0), axis=0, keepdims=True)
    out_ref[...] = jnp.broadcast_to(line, out_ref.shape)


def pair_nt(left, right):
    return lax.dot_general(left, right, (((1,), (1,)), ((), ())), preferred_element_type=F32)


def start_kernel(
    layers, entries, owners, sums_ref, grad_ref, mom_ref, start_ref, keep_ref, send_ref, fac_ref, pack
):
    place = lax.axis_index("dp")
    chip, core, section = place >> 1, place & 1, lax.axis_index("section")
    lane = lax.broadcasted_iota(jnp.int32, (1, sums_ref.shape[1]), 1)
    every = jnp.sum(sums_ref[...], axis=0, keepdims=True)
    mine = sums_ref[pl.ds(pl.multiple_of(section * owners, 8), owners), :]
    mine = jnp.sum(mine, axis=0, keepdims=True)
    kind = lax.rem(lane, 3)
    total = jnp.sum(jnp.where(kind == 0, every, 0.0), axis=1, keepdims=True)
    factor = clip_rms / jnp.sqrt(total / entries + 1e-06)
    fac_ref[...] = jnp.broadcast_to(factor, fac_ref.shape)
    on_grad = factor * (1.0 + momentum_decay)
    on_mom = momentum_decay * momentum_decay
    cross = 2.0 * (on_grad * on_mom)
    known = mine * jnp.where(
        kind == 0, on_grad * on_grad, jnp.where(kind == 1, cross, on_mom * on_mom)
    )

    def visit(layer):
        here = (lane >= 3 * layer) & (lane < 3 * layer + 3)
        guess = jnp.maximum(jnp.sum(jnp.where(here, known, 0.0), axis=1, keepdims=True), 0.0)
        scale = 1.0 / (jnp.sqrt(guess) + 1e-07)
        scaled = factor * grad_ref[layer].astype(F32)
        fresh = momentum_decay * mom_ref[layer] + scaled
        nesterov = (scaled + momentum_decay * fresh).astype(BF16).astype(F32)
        squares = total_of(nesterov * nesterov)
        start = (nesterov * scale).astype(BF16)
        start_ref[layer] = start
        width = start.shape[0]
        tail = width - 2 * LANES
        a, b = LANES, 2 * LANES
        gram = pair_nt(start[0:b], start[0:b])
        edge = pair_nt(start[b:], start)
        hold = pack.at[lax.rem(layer, 2)]
        hold[0:a, :] = gram[0:a, 0:a]
        hold[a:b, :] = gram[0:a, a:b]
        hold[b : b + a, :] = gram[a:b, a:b]
        at = b + a
        hold[at : at + tail, :] = edge[:, 0:a]
        hold[at + tail : at + 2 * tail, :] = edge[:, a:b]
        spot = lax.broadcasted_iota(jnp.int32, (tail, LANES), 1)
        extra = jnp.where(spot == 64, squares, 0.0) + jnp.where(spot == 65, guess, 0.0)
        hold[at + 2 * tail :, :] = extra
        hold[at + 2 * tail :, 0:tail] = edge[:, b:]
        half = pack.shape[1] // 2
        keep_ref[layer ^ chip] = hold[pl.ds(pl.multiple_of(core * half, 8), half), :]
        send_ref[layer ^ chip] = hold[pl.ds(pl.multiple_of((1 - core) * half, 8), half), :]

    over(layers, visit)


def split(value):
    high = value.astype(BF16)
    return high, (value - high.astype(F32)).astype(BF16)


def dot(left, right):
    return jnp.dot(left, right, preferred_element_type=F32)


def wide_left(left, right):
    high, low = split(left)
    b = 2 * LANES
    ends = jnp.concatenate([high[:, b:], low[:, b:]], axis=1)
    rest = jnp.concatenate([right[b:], right[b:]], axis=0)
    return dot(high[:, :b], right[:b]) + dot(low[:, :b], right[:b]) + dot(ends, rest)


def wide_right(left, right):
    high, low = split(right)
    b = 2 * LANES
    ends = jnp.concatenate([left[:, b:], left[:, b:]], axis=1)
    rest = jnp.concatenate([high[b:], low[b:]], axis=0)
    return dot(left[:, :b], high[:b]) + dot(left[:, :b], low[:b]) + dot(ends, rest)


def newton_kernel(owners, width, scal_ref, own_ref, other_ref, mine_ref, theirs_ref, pack, full):
    core = scal_ref[1]
    half = own_ref.shape[0]
    pack[pl.ds(pl.multiple_of(core * half, 8), half), :] = own_ref[...]
    pack[pl.ds(pl.multiple_of((1 - core) * half, 8), half), :] = other_ref[...]
    tail = width - 2 * LANES
    a, b = LANES, 2 * LANES
    at = b + a
    t00, t01, t11 = pack[0:a, :], pack[a:b, :], pack[b:at, :]
    t20, t21 = pack[at : at + tail, :], pack[at + tail : at + 2 * tail, :]
    last = pack[at + 2 * tail :, :]
    t22 = last[:, 0:tail]
    squares = last[0:1, 64:65]
    guess = last[0:1, 65:66] * (1.0 / owners)
    ratio = (jnp.sqrt(guess) + 1e-07) / (jnp.sqrt(squares) + 1e-07)
    gram = jnp.concatenate(
        [
            jnp.concatenate([t00, t01, t20.T], axis=1),
            jnp.concatenate([t01.T, t11, t21.T], axis=1),
            jnp.concatenate([t20, t21, t22], axis=1),
        ],
        axis=0,
    )
    gram = gram * (ratio * ratio)
    ca, cb, cc = newton_coeffs
    rows = lax.broadcasted_iota(jnp.int32, (width, width), 0)
    cols = lax.broadcasted_iota(jnp.int32, (width, width), 1)
    prod = None
    mean_sq = None
    for step in range(NS_STEPS):
        rounded = gram.astype(BF16)
        mix = (cb * rounded.astype(F32) + cc * dot(rounded, rounded)).astype(BF16)
        mix32 = mix.astype(F32)
        turned = ca * gram + wide_left(gram, mix)
        if step < NS_STEPS - 1:
            gram = ca * turned + wide_right(mix, turned)
        else:
            diagonal = jnp.where(rows == cols, turned, 0.0)
            mean_sq = total_of(ca * diagonal + mix32 * turned) * (1.0 / width)
        if prod is None:
            prod = ratio * (jnp.where(rows == cols, ca, 0.0) + mix32)
        else:
            prod = ca * prod + wide_right(mix, prod)
    full[0:width, :] = prod[:, 0:a]
    full[width : 2 * width, :] = prod[:, a:b]
    group = width * tail // LANES
    for i in range(LANES // tail):
        full[2 * width : 2 * width + group, i * tail : (i + 1) * tail] = prod[i * group : (i + 1) * group, b:]
    full[2 * width + group :, :] = jnp.broadcast_to(mean_sq, (8, LANES))
    half = mine_ref.shape[0]
    mine_ref[...] = full[pl.ds(pl.multiple_of(core * half, 8), half), :]
    theirs_ref[...] = full[pl.ds(pl.multiple_of((1 - core) * half, 8), half), :]


def update_kernel(scale, width, rel, final, *refs):
    scal_ref, owner_ref, start_ref, mine_ref, other_ref = refs[:5]
    if rel == 0:
        out_ref, means_out, slot_ref, full = refs[5:]
    else:
        means_ref, _, out_ref, means_out, slot_ref, full = refs[5:]
    core = scal_ref[1]
    layer = scal_ref[0] ^ rel
    half = mine_ref.shape[0]
    full[pl.ds(pl.multiple_of(core * half, 8), half), :] = mine_ref[...]
    full[pl.ds(pl.multiple_of((1 - core) * half, 8), half), :] = other_ref[...]
    tail = width - 2 * LANES
    b = 2 * LANES
    group = width * tail // LANES
    main = jnp.concatenate([full[0:width, :], full[width : 2 * width, :]], axis=1)
    ends = full[2 * width : 2 * width + group, :]
    ends = jnp.concatenate([ends[:, i * tail : (i + 1) * tail] for i in range(LANES // tail)], axis=0)
    high, low = split(main)
    end_high, end_low = split(ends)
    start = start_ref[0]
    rest = jnp.concatenate([start[b:], start[b:]], axis=0)
    value = dot(high, start[:b]) + dot(low, start[:b])
    value = value + dot(jnp.concatenate([end_high, end_low], axis=1), rest)
    out_ref[0] = (value * scale).astype(BF16)
    lane = lax.broadcasted_iota(jnp.int32, means_out.shape, 1)
    means = jnp.where(lane == layer, full[2 * width + group :, :], 0.0)
    if rel:
        means = means + means_ref[...]
    means_out[...] = means
    if not final:
        for slot in range(MAXOWN):
            slot_ref[0, slot] = 0.0
        return
    layers = owner_ref.shape[1]
    me = scal_ref[3]
    for slot in range(MAXOWN):

        def visit(j, carry):
            seen, at = carry
            hit = owner_ref[0, j] == me
            at = jnp.where(hit & (seen == slot), j, at)
            return seen + jnp.where(hit, 1, 0), at

        _, at = lax.fori_loop(0, layers, visit, (jnp.int32(0), jnp.int32(-1)))
        slot_ref[0, slot] = jnp.sum(jnp.where(lane[0:1] == at, means[0:1], 0.0))


def step(momentum, gradient, assignment):
    _, layers, rows, width = momentum.shape
    owners = lax.axis_size("dp")
    sections = lax.axis_size("section")
    chips = owners // 2
    tail = width - 2 * LANES
    assert chips == layers and chips & (chips - 1) == 0 and LANES % tail == 0 and 3 * layers <= LANES
    everyone = sections * owners
    entries = everyone * layers * rows * width
    mom = jnp.swapaxes(momentum[0], 1, 2)
    grad = jnp.swapaxes(gradient[0], 1, 2)
    place = lax.axis_index("dp")
    scal = jnp.stack([place >> 1, place & 1, lax.axis_index("section"), place]).astype(jnp.int32)

    anywhere = pl.BlockSpec(memory_space=pl.ANY)
    near_by = pl.BlockSpec(memory_space=pltpu.VMEM)
    sums, grad_near, mom_near = pl.pallas_call(
        functools.partial(sums_kernel, layers),
        in_specs=[anywhere, anywhere],
        out_specs=[near_by] * 3,
        out_shape=[
            jax.ShapeDtypeStruct((everyone, LANES), F32),
            jax.ShapeDtypeStruct(grad.shape, BF16),
            jax.ShapeDtypeStruct(mom.shape, F32),
        ],
        scratch_shapes=[
            pltpu.VMEM((-(-3 * layers // 8) * 8, rows), F32),
            pltpu.SemaphoreType.DMA((layers, 2)),
        ],
        compiler_params=params(),
        name="sums",
    )(pltpu.with_memory_space_constraint(grad, pltpu.HBM), pltpu.with_memory_space_constraint(mom, pltpu.HBM))
    sums = lax.all_to_all(sums, ("section", "dp"), 0, 0, tiled=True)

    packed = 3 * LANES + 3 * tail
    half = packed // 2
    start, keep, send, factor = pl.pallas_call(
        functools.partial(start_kernel, layers, entries, owners),
        in_specs=[near_by] * 3,
        out_specs=[near_by] * 4,
        out_shape=[
            jax.ShapeDtypeStruct((layers, width, rows), BF16),
            jax.ShapeDtypeStruct((layers, half, LANES), F32),
            jax.ShapeDtypeStruct((layers, half, LANES), F32),
            jax.ShapeDtypeStruct((8, LANES), F32),
        ],
        scratch_shapes=[pltpu.VMEM((2, packed, LANES), F32)],
        compiler_params=params(),
        name="start",
    )(sums, grad_near, mom_near)

    def turn(value, by):
        return lax.ppermute(value, "dp", [(i, i ^ by) for i in range(owners)])

    chip_sums = keep + turn(send, 1)
    own = chip_sums[0]
    for rel in range(1, chips):
        own = own + turn(chip_sums[rel], 2 * rel)
    fresh = momentum_decay * mom_near + factor[0, 0] * grad_near.astype(F32)
    own, fresh = lax.optimization_barrier((own, fresh))
    other = turn(own, 1)

    full_rows = 2 * width + width * tail // LANES + 8
    piece = full_rows // 2
    mine, theirs = pl.pallas_call(
        functools.partial(newton_kernel, owners, width),
        grid_spec=pltpu.PrefetchScalarGridSpec(
            num_scalar_prefetch=1,
            grid=(1,),
            in_specs=[whole((half, LANES)), whole((half, LANES))],
            out_specs=[whole((piece, LANES)), whole((piece, LANES))],
            scratch_shapes=[pltpu.VMEM((packed, LANES), F32), pltpu.VMEM((full_rows, LANES), F32)],
        ),
        out_shape=[jax.ShapeDtypeStruct((piece, LANES), F32)] * 2,
        compiler_params=params(),
        name="newton",
    )(scal, own, other)

    update = means = slots = None
    flops = 4 * width * width * rows
    for rel in range(chips):
        if rel:
            near = arriving[rel]
            if rel < chips - 1:
                near, update = lax.optimization_barrier((near, update))
            far = turn(near, 1)
        else:
            arriving = {}
            for k in range(1, chips):
                arriving[k] = turn(mine, 2 * k)
            near, far = mine, theirs
        pick = pl.BlockSpec((1, width, rows), lambda k, s, _, rel=rel: (s[0] ^ rel, 0, 0))
        operands = [scal, assignment, start, near, far]
        in_specs = [pick, whole((piece, LANES)), whole((piece, LANES))]
        aliases = {}
        if rel:
            operands += [means, update]
            in_specs += [whole((8, LANES)), pl.BlockSpec(memory_space=pl.ANY)]
            aliases = {6: 0}
        call = pl.pallas_call(
            functools.partial(
                update_kernel, math.sqrt(owners * rows), width, rel, rel == chips - 1
            ),
            grid_spec=pltpu.PrefetchScalarGridSpec(
                num_scalar_prefetch=2,
                grid=(1,),
                in_specs=in_specs,
                out_specs=[
                    pick,
                    whole((8, LANES)),
                    pl.BlockSpec((1, MAXOWN), lambda *_: (0, 0), memory_space=pltpu.SMEM),
                ],
                scratch_shapes=[pltpu.VMEM((full_rows, LANES), F32)],
            ),
            out_shape=[
                jax.ShapeDtypeStruct((layers, width, rows), BF16),
                jax.ShapeDtypeStruct((8, LANES), F32),
                jax.ShapeDtypeStruct((1, MAXOWN), F32),
            ],
            input_output_aliases=aliases,
            compiler_params=params(),
            cost_estimate=cost(flops, 4 * width * rows + 8 * piece * LANES),
            name="update",
        )
        update, means, slots = call(*operands)
    return (jnp.swapaxes(fresh, 1, 2)[None], jnp.swapaxes(update, 1, 2)[None], slots)


def solution(mesh):
    in_specs = (P("section", None, "dp", None), P("section", None, "dp", None), P("section", None))
    out_specs = (P("section", None, "dp", None), P("section", None, "dp", None), P("section", "dp"))
    return jax.shard_map(step, mesh=mesh, in_specs=in_specs, out_specs=out_specs, check_vma=False)
```

```python
import functools
import math

import jax
import jax.numpy as jnp
from jax import lax
from jax.experimental import pallas as pl
from jax.experimental.pallas import tpu as pltpu
from jax.sharding import PartitionSpec as P


MAXOWN = 2
NS_STEPS = 5
LANES = 128

momentum_decay = 0.95
clip_rms = 0.5
newton_coeffs = (3.4445, -4.775, 2.0315)

F32 = jnp.float32
BF16 = jnp.bfloat16


VMEM_BYTES = 12 * 2**20


def params():
    return pltpu.CompilerParams(vmem_limit_bytes=VMEM_BYTES)


def cost(flops, bytes_accessed):
    return pl.CostEstimate(flops=flops, bytes_accessed=bytes_accessed, transcendentals=0)


def over(count, visit):
    if count <= 8:
        for i in range(count):
            visit(i)
    else:
        pl.loop(0, count)(visit)


def total_of(values):
    return jnp.sum(jnp.sum(values, axis=0, keepdims=True), axis=1, keepdims=True)


def sums_kernel(layers, grad_in, mom_in, out_ref, grad_ref, mom_ref, acc, sems):
    def copies(layer):
        return (
            pltpu.make_async_copy(grad_in.at[layer], grad_ref.at[layer], sems.at[layer, 0]),
            pltpu.make_async_copy(mom_in.at[layer], mom_ref.at[layer], sems.at[layer, 1]),
        )

    def begin(layer):
        for copy in copies(layer):
            copy.start()

    def visit(layer):
        for copy in copies(layer):
            copy.wait()
        grads = grad_ref[layer].astype(F32)
        moms = mom_ref[layer]
        for i, prod in enumerate((grads * grads, grads * moms, moms * moms)):
            acc[pl.ds(3 * layer + i, 1), :] = jnp.sum(prod, axis=0, keepdims=True)

    acc[...] = jnp.zeros_like(acc)
    over(layers, begin)
    over(layers, visit)
    column = jnp.sum(acc[...], axis=1, keepdims=True)
    shape = (acc.shape[0], out_ref.shape[1])
    hit = lax.broadcasted_iota(jnp.int32, shape, 0) == lax.broadcasted_iota(jnp.int32, shape, 1)
    line = jnp.sum(jnp.where(hit, column, 0.0), axis=0, keepdims=True)
    out_ref[...] = jnp.broadcast_to(line, out_ref.shape)


def pair_nt(left, right):
    return lax.dot_general(left, right, (((1,), (1,)), ((), ())), preferred_element_type=F32)


def start_kernel(
    layers, entries, owners, sums_ref, grad_ref, mom_ref, start_ref, keep_ref, send_ref, fac_ref, pack
):
    place = lax.axis_index("dp")
    chip, core, section = place >> 1, place & 1, lax.axis_index("section")
    lane = lax.broadcasted_iota(jnp.int32, (1, sums_ref.shape[1]), 1)
    every = jnp.sum(sums_ref[...], axis=0, keepdims=True)
    mine = sums_ref[pl.ds(pl.multiple_of(section * owners, 8), owners), :]
    mine = jnp.sum(mine, axis=0, keepdims=True)
    kind = lax.rem(lane, 3)
    total = jnp.sum(jnp.where(kind == 0, every, 0.0), axis=1, keepdims=True)
    factor = clip_rms / jnp.sqrt(total / entries + 1e-06)
    fac_ref[...] = jnp.broadcast_to(factor, fac_ref.shape)
    on_grad = factor * (1.0 + momentum_decay)
    on_mom = momentum_decay * momentum_decay
    cross = 2.0 * (on_grad * on_mom)
    known = mine * jnp.where(
        kind == 0, on_grad * on_grad, jnp.where(kind == 1, cross, on_mom * on_mom)
    )

    def visit(layer):
        here = (lane >= 3 * layer) & (lane < 3 * layer + 3)
        guess = jnp.maximum(jnp.sum(jnp.where(here, known, 0.0), axis=1, keepdims=True), 0.0)
        scale = 1.0 / (jnp.sqrt(guess) + 1e-07)
        scaled = factor * grad_ref[layer].astype(F32)
        fresh = momentum_decay * mom_ref[layer] + scaled
        nesterov = (scaled + momentum_decay * fresh).astype(BF16).astype(F32)
        squares = total_of(nesterov * nesterov)
        start = (nesterov * scale).astype(BF16)
        start_ref[layer] = start
        width = start.shape[0]
        tail = width - 2 * LANES
        a, b = LANES, 2 * LANES
        gram = pair_nt(start[0:b], start[0:b])
        edge = pair_nt(start[b:], start)
        hold = pack.at[lax.rem(layer, 2)]
        down, across = grid_of(LANES)
        t11 = gram[a:b, a:b]
        hold[0:a, :] = jnp.where(down >= across, gram[0:a, 0:a], t11)
        hold[a:b, :] = gram[0:a, a:b]
        hold[b : b + tail, :] = edge[:, 0:a]
        hold[b + tail : b + 2 * tail, :] = edge[:, a:b]
        at = b + 2 * tail
        small = tail * tail // LANES
        lay_corner(hold, at, edge[:, b:])
        diagonal = jnp.sum(jnp.where(down == across, t11, 0.0), axis=0, keepdims=True)
        row, spot = lax.broadcasted_iota(jnp.int32, (8, LANES), 0), lax.broadcasted_iota(jnp.int32, (8, LANES), 1)
        extra = jnp.where(spot == 0, squares, jnp.where(spot == 1, guess, 0.0))
        hold[at + small :, :] = jnp.where(row == 0, diagonal, extra)
        half = pack.shape[1] // 2
        keep_ref[layer ^ chip] = hold[pl.ds(pl.multiple_of(core * half, 8), half), :]
        send_ref[layer ^ chip] = hold[pl.ds(pl.multiple_of((1 - core) * half, 8), half), :]

    over(layers, visit)


def grid_of(size):
    return lax.broadcasted_iota(jnp.int32, (size, size), 0), lax.broadcasted_iota(jnp.int32, (size, size), 1)


def packed_rows(tail):
    return 2 * LANES + 2 * tail + tail * tail // LANES + 8


def lay_corner(hold, at, block):
    tail = block.shape[1]
    small = tail * tail // LANES
    for i in range(LANES // tail):
        hold[at : at + small, i * tail : (i + 1) * tail] = block[i * small : (i + 1) * small]


def read_corner(block, tail):
    return jnp.concatenate([block[:, i * tail : (i + 1) * tail] for i in range(LANES // tail)], axis=0)


def half_of(ref, core, half, align=8):
    return ref.at[pl.ds(pl.multiple_of(core * half, align), half)]


def sent_rows(tail):
    return -(-3 * packed_rows(tail) // 32) * 32


def split(value):
    high = value.astype(BF16)
    return high, (value - high.astype(F32)).astype(BF16)


def dot(left, right):
    return jnp.dot(left, right, preferred_element_type=F32)


def wide_left(left, right):
    high, low = split(left)
    b = 2 * LANES
    ends = jnp.concatenate([high[:, b:], low[:, b:]], axis=1)
    rest = jnp.concatenate([right[b:], right[b:]], axis=0)
    return dot(high[:, :b], right[:b]) + dot(low[:, :b], right[:b]) + dot(ends, rest)


def wide_right(left, right):
    high, low = split(right)
    b = 2 * LANES
    ends = jnp.concatenate([left[:, b:], left[:, b:]], axis=1)
    rest = jnp.concatenate([high[b:], low[b:]], axis=0)
    return dot(left[:, :b], high[:b]) + dot(left[:, :b], low[:b]) + dot(ends, rest)


def newton_kernel(owners, width, own_ref, other_ref, mine_ref, theirs_ref, pack, skew, full):
    core = lax.axis_index("dp") & 1
    half = own_ref.shape[0]
    pack[pl.ds(pl.multiple_of(core * half, 8), half), :] = own_ref[...]
    pack[pl.ds(pl.multiple_of((1 - core) * half, 8), half), :] = other_ref[...]
    tail = width - 2 * LANES
    a, b = LANES, 2 * LANES
    merged, t01 = pack[0:a, :], pack[a:b, :]
    t20, t21 = pack[b : b + tail, :], pack[b + tail : b + 2 * tail, :]
    at = b + 2 * tail
    small = tail * tail // LANES
    t22 = read_corner(pack[at : at + small, :], tail)
    extra = pack[at + small :, :]
    down, across = grid_of(LANES)
    flipped = merged.T
    t00 = jnp.where(down >= across, merged, flipped)
    t11 = jnp.where(down == across, extra[0:1, :], jnp.where(down < across, merged, flipped))
    squares = extra[1:2, 0:1]
    guess = extra[1:2, 1:2] * (1.0 / owners)
    ratio = (jnp.sqrt(guess) + 1e-07) / (jnp.sqrt(squares) + 1e-07)
    gram = jnp.concatenate(
        [
            jnp.concatenate([t00, t01, t20.T], axis=1),
            jnp.concatenate([t01.T, t11, t21.T], axis=1),
            jnp.concatenate([t20, t21, t22], axis=1),
        ],
        axis=0,
    )
    gram = gram * (ratio * ratio)
    ca, cb, cc = newton_coeffs
    rows = lax.broadcasted_iota(jnp.int32, (width, width), 0)
    cols = lax.broadcasted_iota(jnp.int32, (width, width), 1)
    prod = None
    mean_sq = None
    for step in range(NS_STEPS):
        rounded = gram.astype(BF16)
        mix = (cb * rounded.astype(F32) + cc * dot(rounded, rounded)).astype(BF16)
        mix32 = mix.astype(F32)
        turned = ca * gram + wide_left(gram, mix)
        if step < NS_STEPS - 1:
            gram = ca * turned + wide_right(mix, turned)
        else:
            diagonal = jnp.where(rows == cols, turned, 0.0)
            mean_sq = total_of(ca * diagonal + mix32 * turned) * (1.0 / width)
        if prod is None:
            prod = ratio * (jnp.where(rows == cols, ca, 0.0) + mix32)
        else:
            prod = ca * prod + wide_right(mix, prod)
    p00, p11 = prod[0:a, 0:a], prod[a:b, a:b]
    back00, back11 = p00.T, p11.T
    p01, back10 = prod[0:a, a:b], prod[a:b, 0:a].T
    p2, back2 = prod[b:, 0:b], prod[0:b, b:].T
    p22 = prod[b:, b:]
    lower = down >= across
    for ref, sign in ((pack, 1.0), (skew, -1.0)):
        ref[0:a, :] = 0.5 * jnp.where(lower, p00 + sign * back00, p11 + sign * back11)
        ref[a:b, :] = 0.5 * (p01 + sign * back10)
        edge = 0.5 * (p2 + sign * back2)
        ref[b : b + tail, :] = edge[:, 0:a]
        ref[b + tail : at, :] = edge[:, a:b]
        lay_corner(ref, at, p22 if ref is pack else jnp.zeros_like(p22))
    diagonal = jnp.sum(jnp.where(down == across, p11, 0.0), axis=0, keepdims=True)
    first = lax.broadcasted_iota(jnp.int32, (8, LANES), 0) == 0
    pack[at + small :, :] = jnp.where(first, diagonal, mean_sq)
    skew[at + small :, :] = jnp.zeros((8, LANES), F32)
    rows = pack.shape[0]
    high, low = split(pack[...])
    full[0:rows, :] = high
    full[rows : 2 * rows, :] = low
    full[2 * rows : 3 * rows, :] = skew[...].astype(BF16)
    if full.shape[0] > 3 * rows:
        full[3 * rows :, :] = jnp.zeros((full.shape[0] - 3 * rows, LANES), BF16)
    half = mine_ref.shape[0]
    mine_ref[...] = half_of(full, core, half, 16)[...]
    theirs_ref[...] = half_of(full, 1 - core, half, 16)[...]


def update_kernel(scale, width, group, last, *refs):
    owner_ref, start_ref = refs[:2]
    products = refs[2 : 2 + 2 * len(group)]
    refs = refs[2 + 2 * len(group) :]
    means = None
    if group[0]:
        means = refs[0][...]
        refs = refs[2:]
    slot_ref = None
    if last:
        slot_ref, refs = refs[2], refs[:2] + refs[3:]
    out_ref, means_out, fulls, values, sems = refs
    place = lax.axis_index("dp")
    chip, core = place >> 1, place & 1
    tail = width - 2 * LANES
    b = 2 * LANES
    down, across = grid_of(LANES)
    lane = lax.broadcasted_iota(jnp.int32, means_out.shape, 1)
    copies = []
    for i, rel in enumerate(group):
        layer = chip ^ rel
        mine_ref, other_ref = products[2 * i : 2 * i + 2]
        full = fulls.at[i]
        half = mine_ref.shape[0]
        half_of(full, core, half, 16)[...] = mine_ref[...]
        half_of(full, 1 - core, half, 16)[...] = other_ref[...]
        size = packed_rows(tail)
        even = full[0:size, :].astype(F32) + full[size : 2 * size, :].astype(F32)
        odd = full[2 * size : 3 * size, :].astype(F32)
        plus, minus = even + odd, even - odd
        at = b + 2 * tail
        small = tail * tail // LANES
        extra = even[at + small :]
        turned = minus[0:LANES].T
        p00 = jnp.where(down >= across, plus[0:LANES], turned)
        p11 = jnp.where(
            down == across, extra[0:1], jnp.where(down < across, plus[0:LANES], turned)
        )
        p10 = minus[LANES:b].T
        main = jnp.concatenate(
            [
                jnp.concatenate([p00, plus[LANES:b]], axis=1),
                jnp.concatenate([p10, p11], axis=1),
                jnp.concatenate([plus[b : b + tail], plus[b + tail : at]], axis=1),
            ],
            axis=0,
        )
        ends = jnp.concatenate(
            [minus[b : b + tail].T, minus[b + tail : at].T, read_corner(even[at : at + small], tail)],
            axis=0,
        )
        high, low = split(main)
        end_high, end_low = split(ends)
        start = start_ref[layer]
        rest = jnp.concatenate([start[b:], start[b:]], axis=0)
        value = dot(high, start[:b]) + dot(low, start[:b])
        value = value + dot(jnp.concatenate([end_high, end_low], axis=1), rest)
        values[i] = (value * scale).astype(BF16)
        copies.append(
            pltpu.make_async_copy(values.at[i], out_ref.at[layer], sems.at[i])
        )
        copies[-1].start()
        found = jnp.where(lane == layer, extra[1:2], 0.0)
        means = found if means is None else means + found
    means_out[...] = means
    if last:
        for slot in range(MAXOWN):

            def visit(j, carry):
                seen, at = carry
                hit = owner_ref[0, j] == place
                at = jnp.where(hit & (seen == slot), j, at)
                return seen + jnp.where(hit, 1, 0), at

            _, at = lax.fori_loop(0, owner_ref.shape[1], visit, (jnp.int32(0), jnp.int32(-1)))
            slot_ref[0, slot] = jnp.sum(jnp.where(lane[0:1] == at, means[0:1], 0.0))
    for copy in copies:
        copy.wait()


def step(momentum, gradient, assignment):
    _, layers, rows, width = momentum.shape
    owners = lax.axis_size("dp")
    sections = lax.axis_size("section")
    chips = owners // 2
    tail = width - 2 * LANES
    assert chips == layers and chips & (chips - 1) == 0 and LANES % tail == 0 and 3 * layers <= LANES
    everyone = sections * owners
    entries = everyone * layers * rows * width
    mom = jnp.swapaxes(momentum[0], 1, 2)
    grad = jnp.swapaxes(gradient[0], 1, 2)
    anywhere = pl.BlockSpec(memory_space=pl.ANY)
    near_by = pl.BlockSpec(memory_space=pltpu.VMEM)
    sums, grad_near, mom_near = pl.pallas_call(
        functools.partial(sums_kernel, layers),
        in_specs=[anywhere, anywhere],
        out_specs=[near_by] * 3,
        out_shape=[
            jax.ShapeDtypeStruct((everyone, LANES), F32),
            jax.ShapeDtypeStruct(grad.shape, BF16),
            jax.ShapeDtypeStruct(mom.shape, F32),
        ],
        scratch_shapes=[
            pltpu.VMEM((-(-3 * layers // 8) * 8, rows), F32),
            pltpu.SemaphoreType.DMA((layers, 2)),
        ],
        compiler_params=params(),
        name="sums",
    )(pltpu.with_memory_space_constraint(grad, pltpu.HBM), pltpu.with_memory_space_constraint(mom, pltpu.HBM))
    sums = lax.all_to_all(sums, ("section", "dp"), 0, 0, tiled=True)

    packed = packed_rows(tail)
    half = packed // 2
    start, keep, send, factor = pl.pallas_call(
        functools.partial(start_kernel, layers, entries, owners),
        in_specs=[near_by] * 3,
        out_specs=[near_by] * 4,
        out_shape=[
            jax.ShapeDtypeStruct((layers, width, rows), BF16),
            jax.ShapeDtypeStruct((layers, half, LANES), F32),
            jax.ShapeDtypeStruct((layers, half, LANES), F32),
            jax.ShapeDtypeStruct((8, LANES), F32),
        ],
        scratch_shapes=[pltpu.VMEM((2, packed, LANES), F32)],
        compiler_params=params(),
        name="start",
    )(sums, grad_near, mom_near)

    def turn(value, by):
        return lax.ppermute(value, "dp", [(i, i ^ by) for i in range(owners)])

    chip_sums = keep + turn(send, 1)
    own = chip_sums[0]
    for rel in range(1, chips):
        own = own + turn(chip_sums[rel], 2 * rel)
    fresh = momentum_decay * mom_near + factor[0, 0] * grad_near.astype(F32)
    own, fresh = lax.optimization_barrier((own, fresh))
    other = turn(own, 1)

    full_rows = sent_rows(tail)
    piece = full_rows // 2
    mine, theirs = pl.pallas_call(
        functools.partial(newton_kernel, owners, width),
        in_specs=[near_by] * 2,
        out_specs=[near_by] * 2,
        out_shape=[jax.ShapeDtypeStruct((piece, LANES), BF16)] * 2,
        scratch_shapes=[
            pltpu.VMEM((packed, LANES), F32),
            pltpu.VMEM((packed, LANES), F32),
            pltpu.VMEM((full_rows, LANES), BF16),
        ],
        compiler_params=params(),
        name="newton",
    )(own, other)

    arriving = {}
    for k in range(1, chips):
        arriving[k] = turn(mine, 2 * k)
    update = means = slots = None
    flops = 4 * width * width * rows
    groups = [(0,), (1,)] + [tuple(range(k, min(k + 2, chips))) for k in range(2, chips, 2)]
    for group in groups:
        last = group[-1] == chips - 1
        operands = [assignment, start]
        if group[0]:
            nears, update = lax.optimization_barrier(([arriving[rel] for rel in group], update))
            for near in nears:
                operands += [near, turn(near, 1)]
        else:
            operands += [mine, theirs]
        in_specs = [pl.BlockSpec(memory_space=pltpu.SMEM)] + [near_by] * (len(operands) - 1)
        aliases = {}
        if group[0]:
            aliases = {len(operands) + 1: 0}
            operands += [means, update]
            in_specs += [near_by, pl.BlockSpec(memory_space=pl.ANY)]
        call = pl.pallas_call(
            functools.partial(update_kernel, math.sqrt(owners * rows), width, group, last),
            in_specs=in_specs,
            out_specs=[pl.BlockSpec(memory_space=pl.ANY), near_by]
            + [pl.BlockSpec(memory_space=pltpu.SMEM)] * last,
            out_shape=[
                jax.ShapeDtypeStruct((layers, width, rows), BF16),
                jax.ShapeDtypeStruct((8, LANES), F32),
            ]
            + [jax.ShapeDtypeStruct((1, MAXOWN), F32)] * last,
            scratch_shapes=[
                pltpu.VMEM((len(group), full_rows, LANES), BF16),
                pltpu.VMEM((len(group), width, rows), BF16),
                pltpu.SemaphoreType.DMA((len(group),)),
            ],
            input_output_aliases=aliases,
            compiler_params=params(),
            cost_estimate=cost(
                len(group) * flops, len(group) * (4 * width * rows + 4 * piece * LANES)
            ),
            name="update",
        )
        update, means, *slots = call(*operands)
    return (jnp.swapaxes(fresh, 1, 2)[None], jnp.swapaxes(update, 1, 2)[None], slots[0])


def solution(mesh):
    in_specs = (P("section", None, "dp", None), P("section", None, "dp", None), P("section", None))
    out_specs = (P("section", None, "dp", None), P("section", None, "dp", None), P("section", "dp"))
    return jax.shard_map(step, mesh=mesh, in_specs=in_specs, out_specs=out_specs, check_vma=False)
```

```python
import functools
import math

import jax
import jax.numpy as jnp
from jax import lax
from jax.experimental import pallas as pl
from jax.experimental.pallas import tpu as pltpu
from jax.sharding import PartitionSpec as P


MAXOWN = 2
NS_STEPS = 5
LANES = 128

momentum_decay = 0.95
clip_rms = 0.5
newton_coeffs = (3.4445, -4.775, 2.0315)

F32 = jnp.float32
BF16 = jnp.bfloat16


VMEM_BYTES = 12 * 2**20


def params():
    return pltpu.CompilerParams(vmem_limit_bytes=VMEM_BYTES)


def cost(flops, bytes_accessed):
    return pl.CostEstimate(flops=flops, bytes_accessed=bytes_accessed, transcendentals=0)


def over(count, visit):
    if count <= 8:
        for i in range(count):
            visit(i)
    else:
        pl.loop(0, count)(visit)


def total_of(values):
    return jnp.sum(jnp.sum(values, axis=0, keepdims=True), axis=1, keepdims=True)


def sums_kernel(layers, grad_in, mom_in, out_ref, grad_ref, mom_ref, acc, sems):
    def copies(layer):
        return (
            pltpu.make_async_copy(grad_in.at[layer], grad_ref.at[layer], sems.at[layer, 0]),
            pltpu.make_async_copy(mom_in.at[layer], mom_ref.at[layer], sems.at[layer, 1]),
        )

    def begin(layer):
        for copy in copies(layer):
            copy.start()

    def visit(layer):
        for copy in copies(layer):
            copy.wait()
        grads = grad_ref[layer].astype(F32)
        moms = mom_ref[layer]
        for i, prod in enumerate((grads * grads, grads * moms, moms * moms)):
            acc[pl.ds(3 * layer + i, 1), :] = jnp.sum(prod, axis=0, keepdims=True)

    acc[...] = jnp.zeros_like(acc)
    over(layers, begin)
    over(layers, visit)
    column = jnp.sum(acc[...], axis=1, keepdims=True)
    shape = (acc.shape[0], out_ref.shape[1])
    hit = lax.broadcasted_iota(jnp.int32, shape, 0) == lax.broadcasted_iota(jnp.int32, shape, 1)
    line = jnp.sum(jnp.where(hit, column, 0.0), axis=0, keepdims=True)
    out_ref[...] = jnp.broadcast_to(line, out_ref.shape)


def pair_nt(left, right):
    return lax.dot_general(left, right, (((1,), (1,)), ((), ())), preferred_element_type=F32)


def start_kernel(
    layers, entries, owners, sums_ref, grad_ref, mom_ref, start_ref, keep_ref, send_ref, fac_ref, pack
):
    place = lax.axis_index("dp")
    chip, core, section = place >> 1, place & 1, lax.axis_index("section")
    lane = lax.broadcasted_iota(jnp.int32, (1, sums_ref.shape[1]), 1)
    every = jnp.sum(sums_ref[...], axis=0, keepdims=True)
    mine = sums_ref[pl.ds(pl.multiple_of(section * owners, 8), owners), :]
    mine = jnp.sum(mine, axis=0, keepdims=True)
    kind = lax.rem(lane, 3)
    total = jnp.sum(jnp.where(kind == 0, every, 0.0), axis=1, keepdims=True)
    factor = clip_rms / jnp.sqrt(total / entries + 1e-06)
    fac_ref[...] = jnp.broadcast_to(factor, fac_ref.shape)
    on_grad = factor * (1.0 + momentum_decay)
    on_mom = momentum_decay * momentum_decay
    cross = 2.0 * (on_grad * on_mom)
    known = mine * jnp.where(
        kind == 0, on_grad * on_grad, jnp.where(kind == 1, cross, on_mom * on_mom)
    )

    def visit(layer):
        here = (lane >= 3 * layer) & (lane < 3 * layer + 3)
        guess = jnp.maximum(jnp.sum(jnp.where(here, known, 0.0), axis=1, keepdims=True), 0.0)
        scale = 1.0 / (jnp.sqrt(guess) + 1e-07)
        scaled = factor * grad_ref[layer].astype(F32)
        fresh = momentum_decay * mom_ref[layer] + scaled
        nesterov = (scaled + momentum_decay * fresh).astype(BF16).astype(F32)
        squares = total_of(nesterov * nesterov)
        start = (nesterov * scale).astype(BF16)
        start_ref[layer] = start
        width = start.shape[0]
        tail = width - 2 * LANES
        a, b = LANES, 2 * LANES
        gram = pair_nt(start[0:b], start[0:b])
        edge = pair_nt(start[b:], start)
        hold = pack.at[lax.rem(layer, 2)]
        down, across = grid_of(LANES)
        t11 = gram[a:b, a:b]
        hold[0:a, :] = jnp.where(down >= across, gram[0:a, 0:a], t11)
        hold[a:b, :] = gram[0:a, a:b]
        hold[b : b + tail, :] = edge[:, 0:a]
        hold[b + tail : b + 2 * tail, :] = edge[:, a:b]
        at = b + 2 * tail
        small = tail * tail // LANES
        lay_corner(hold, at, edge[:, b:])
        diagonal = jnp.sum(jnp.where(down == across, t11, 0.0), axis=0, keepdims=True)
        row, spot = lax.broadcasted_iota(jnp.int32, (8, LANES), 0), lax.broadcasted_iota(jnp.int32, (8, LANES), 1)
        extra = jnp.where(spot == 0, squares, jnp.where(spot == 1, guess, 0.0))
        hold[at + small :, :] = jnp.where(row == 0, diagonal, extra)
        half = pack.shape[1] // 2
        keep_ref[layer ^ chip] = hold[pl.ds(pl.multiple_of(core * half, 8), half), :]
        send_ref[layer ^ chip] = hold[pl.ds(pl.multiple_of((1 - core) * half, 8), half), :]

    over(layers, visit)


def grid_of(size):
    return lax.broadcasted_iota(jnp.int32, (size, size), 0), lax.broadcasted_iota(jnp.int32, (size, size), 1)


def packed_rows(tail):
    return 2 * LANES + 2 * tail + tail * tail // LANES + 8


def lay_corner(hold, at, block):
    tail = block.shape[1]
    small = tail * tail // LANES
    for i in range(LANES // tail):
        hold[at : at + small, i * tail : (i + 1) * tail] = block[i * small : (i + 1) * small]


def read_corner(block, tail):
    return jnp.concatenate([block[:, i * tail : (i + 1) * tail] for i in range(LANES // tail)], axis=0)


def half_of(ref, core, half, align=8):
    return ref.at[pl.ds(pl.multiple_of(core * half, align), half)]


def sent_rows(tail):
    return -(-3 * packed_rows(tail) // 32) * 32


def split(value):
    high = value.astype(BF16)
    return high, (value - high.astype(F32)).astype(BF16)


def dot(left, right):
    return jnp.dot(left, right, preferred_element_type=F32)


def wide_left(left, right):
    high, low = split(left)
    b = 2 * LANES
    ends = jnp.concatenate([high[:, b:], low[:, b:]], axis=1)
    rest = jnp.concatenate([right[b:], right[b:]], axis=0)
    return dot(high[:, :b], right[:b]) + dot(low[:, :b], right[:b]) + dot(ends, rest)


def wide_right(left, right):
    high, low = split(right)
    b = 2 * LANES
    ends = jnp.concatenate([left[:, b:], left[:, b:]], axis=1)
    rest = jnp.concatenate([high[b:], low[b:]], axis=0)
    return dot(left[:, :b], high[:b]) + dot(left[:, :b], low[:b]) + dot(ends, rest)


def newton_kernel(owners, width, own_ref, other_ref, mine_ref, theirs_ref, pack, skew, full):
    core = lax.axis_index("dp") & 1
    half = own_ref.shape[0]
    pack[pl.ds(pl.multiple_of(core * half, 8), half), :] = own_ref[...]
    pack[pl.ds(pl.multiple_of((1 - core) * half, 8), half), :] = other_ref[...]
    tail = width - 2 * LANES
    a, b = LANES, 2 * LANES
    merged, t01 = pack[0:a, :], pack[a:b, :]
    t20, t21 = pack[b : b + tail, :], pack[b + tail : b + 2 * tail, :]
    at = b + 2 * tail
    small = tail * tail // LANES
    t22 = read_corner(pack[at : at + small, :], tail)
    extra = pack[at + small :, :]
    down, across = grid_of(LANES)
    flipped = merged.T
    t00 = jnp.where(down >= across, merged, flipped)
    t11 = jnp.where(down == across, extra[0:1, :], jnp.where(down < across, merged, flipped))
    squares = extra[1:2, 0:1]
    guess = extra[1:2, 1:2] * (1.0 / owners)
    ratio = (jnp.sqrt(guess) + 1e-07) / (jnp.sqrt(squares) + 1e-07)
    gram = jnp.concatenate(
        [
            jnp.concatenate([t00, t01, t20.T], axis=1),
            jnp.concatenate([t01.T, t11, t21.T], axis=1),
            jnp.concatenate([t20, t21, t22], axis=1),
        ],
        axis=0,
    )
    gram = gram * (ratio * ratio)
    ca, cb, cc = newton_coeffs
    rows = lax.broadcasted_iota(jnp.int32, (width, width), 0)
    cols = lax.broadcasted_iota(jnp.int32, (width, width), 1)
    prod = None
    mean_sq = None
    for step in range(NS_STEPS):
        rounded = gram.astype(BF16)
        mix = (cb * rounded.astype(F32) + cc * dot(rounded, rounded)).astype(BF16)
        mix32 = mix.astype(F32)
        turned = ca * gram + wide_left(gram, mix)
        if step < NS_STEPS - 1:
            gram = ca * turned + wide_right(mix, turned)
        else:
            diagonal = jnp.where(rows == cols, turned, 0.0)
            mean_sq = total_of(ca * diagonal + mix32 * turned) * (1.0 / width)
        if prod is None:
            prod = ratio * (jnp.where(rows == cols, ca, 0.0) + mix32)
        else:
            prod = ca * prod + wide_right(mix, prod)
    p00, p11 = prod[0:a, 0:a], prod[a:b, a:b]
    back00, back11 = p00.T, p11.T
    p01, back10 = prod[0:a, a:b], prod[a:b, 0:a].T
    p2, back2 = prod[b:, 0:b], prod[0:b, b:].T
    p22 = prod[b:, b:]
    lower = down >= across
    for ref, sign in ((pack, 1.0), (skew, -1.0)):
        ref[0:a, :] = 0.5 * jnp.where(lower, p00 + sign * back00, p11 + sign * back11)
        ref[a:b, :] = 0.5 * (p01 + sign * back10)
        edge = 0.5 * (p2 + sign * back2)
        ref[b : b + tail, :] = edge[:, 0:a]
        ref[b + tail : at, :] = edge[:, a:b]
        lay_corner(ref, at, p22 if ref is pack else jnp.zeros_like(p22))
    diagonal = jnp.sum(jnp.where(down == across, p11, 0.0), axis=0, keepdims=True)
    first = lax.broadcasted_iota(jnp.int32, (8, LANES), 0) == 0
    pack[at + small :, :] = jnp.where(first, diagonal, mean_sq)
    skew[at + small :, :] = jnp.zeros((8, LANES), F32)
    rows = pack.shape[0]
    high, low = split(pack[...])
    full[0:rows, :] = high
    full[rows : 2 * rows, :] = low
    full[2 * rows : 3 * rows, :] = skew[...].astype(BF16)
    if full.shape[0] > 3 * rows:
        full[3 * rows :, :] = jnp.zeros((full.shape[0] - 3 * rows, LANES), BF16)
    half = mine_ref.shape[0]
    mine_ref[...] = half_of(full, core, half, 16)[...]
    theirs_ref[...] = half_of(full, 1 - core, half, 16)[...]


def update_kernel(scale, width, group, last, *refs):
    owner_ref, start_ref = refs[:2]
    products = refs[2 : 2 + 2 * len(group)]
    refs = refs[2 + 2 * len(group) :]
    means = None
    if group[0]:
        means = refs[0][...]
        refs = refs[2:]
    if last:
        out_ref, slot_out, fulls, values, sems, slot_ref, slot_sem = refs
    else:
        out_ref, means_out, fulls, values, sems = refs
    place = lax.axis_index("dp")
    chip, core = place >> 1, place & 1
    tail = width - 2 * LANES
    b = 2 * LANES
    down, across = grid_of(LANES)
    lane = lax.broadcasted_iota(jnp.int32, (8, LANES), 1)
    copies = []
    for i, rel in enumerate(group):
        layer = chip ^ rel
        mine_ref, other_ref = products[2 * i : 2 * i + 2]
        full = fulls.at[i]
        half = mine_ref.shape[0]
        half_of(full, core, half, 16)[...] = mine_ref[...]
        half_of(full, 1 - core, half, 16)[...] = other_ref[...]
        size = packed_rows(tail)
        even = full[0:size, :].astype(F32) + full[size : 2 * size, :].astype(F32)
        odd = full[2 * size : 3 * size, :].astype(F32)
        plus, minus = even + odd, even - odd
        at = b + 2 * tail
        small = tail * tail // LANES
        extra = even[at + small :]
        turned = minus[0:LANES].T
        p00 = jnp.where(down >= across, plus[0:LANES], turned)
        p11 = jnp.where(
            down == across, extra[0:1], jnp.where(down < across, plus[0:LANES], turned)
        )
        p10 = minus[LANES:b].T
        main = jnp.concatenate(
            [
                jnp.concatenate([p00, plus[LANES:b]], axis=1),
                jnp.concatenate([p10, p11], axis=1),
                jnp.concatenate([plus[b : b + tail], plus[b + tail : at]], axis=1),
            ],
            axis=0,
        )
        ends = jnp.concatenate(
            [minus[b : b + tail].T, minus[b + tail : at].T, read_corner(even[at : at + small], tail)],
            axis=0,
        )
        high, low = split(main)
        end_high, end_low = split(ends)
        start = start_ref[layer]
        rest = jnp.concatenate([start[b:], start[b:]], axis=0)
        value = dot(high, start[:b]) + dot(low, start[:b])
        value = value + dot(jnp.concatenate([end_high, end_low], axis=1), rest)
        values[i] = (value * scale).astype(BF16)
        copies.append(
            pltpu.make_async_copy(values.at[i], out_ref.at[layer], sems.at[i])
        )
        copies[-1].start()
        found = jnp.where(lane == layer, extra[1:2], 0.0)
        means = found if means is None else means + found
    if last:
        line = jnp.zeros((1, LANES), F32)
        for slot in range(MAXOWN):

            def visit(j, carry):
                seen, at = carry
                hit = owner_ref[0, j] == place
                at = jnp.where(hit & (seen == slot), j, at)
                return seen + jnp.where(hit, 1, 0), at

            _, at = lax.fori_loop(
                0, owner_ref.shape[1], visit, (jnp.int32(0), jnp.int32(-1)), unroll=owner_ref.shape[1] <= 8
            )
            value = jnp.sum(jnp.where(lane[0:1] == at, means[0:1], 0.0), axis=1, keepdims=True)
            line = jnp.where(lane[0:1] == slot, value, line)
        slot_ref[...] = line[:, 0:MAXOWN]
        copies.append(pltpu.make_async_copy(slot_ref, slot_out, slot_sem))
        copies[-1].start()
    else:
        means_out[...] = means
    for copy in copies:
        copy.wait()


def step(momentum, gradient, assignment):
    _, layers, rows, width = momentum.shape
    owners = lax.axis_size("dp")
    sections = lax.axis_size("section")
    chips = owners // 2
    tail = width - 2 * LANES
    assert chips == layers and chips & (chips - 1) == 0 and LANES % tail == 0 and 3 * layers <= LANES
    everyone = sections * owners
    entries = everyone * layers * rows * width
    mom = jnp.swapaxes(momentum[0], 1, 2)
    grad = jnp.swapaxes(gradient[0], 1, 2)
    anywhere = pl.BlockSpec(memory_space=pl.ANY)
    near_by = pl.BlockSpec(memory_space=pltpu.VMEM)
    sums, grad_near, mom_near = pl.pallas_call(
        functools.partial(sums_kernel, layers),
        in_specs=[anywhere, anywhere],
        out_specs=[near_by] * 3,
        out_shape=[
            jax.ShapeDtypeStruct((everyone, LANES), F32),
            jax.ShapeDtypeStruct(grad.shape, BF16),
            jax.ShapeDtypeStruct(mom.shape, F32),
        ],
        scratch_shapes=[
            pltpu.VMEM((-(-3 * layers // 8) * 8, rows), F32),
            pltpu.SemaphoreType.DMA((layers, 2)),
        ],
        compiler_params=params(),
        name="sums",
    )(pltpu.with_memory_space_constraint(grad, pltpu.HBM), pltpu.with_memory_space_constraint(mom, pltpu.HBM))
    sums = lax.all_to_all(sums, ("section", "dp"), 0, 0, tiled=True)

    packed = packed_rows(tail)
    half = packed // 2
    start, keep, send, factor = pl.pallas_call(
        functools.partial(start_kernel, layers, entries, owners),
        in_specs=[near_by] * 3,
        out_specs=[near_by] * 4,
        out_shape=[
            jax.ShapeDtypeStruct((layers, width, rows), BF16),
            jax.ShapeDtypeStruct((layers, half, LANES), F32),
            jax.ShapeDtypeStruct((layers, half, LANES), F32),
            jax.ShapeDtypeStruct((8, LANES), F32),
        ],
        scratch_shapes=[pltpu.VMEM((2, packed, LANES), F32)],
        compiler_params=params(),
        name="start",
    )(sums, grad_near, mom_near)

    def turn(value, by):
        return lax.ppermute(value, "dp", [(i, i ^ by) for i in range(owners)])

    chip_sums = keep + turn(send, 1)
    own = chip_sums[0]
    for rel in range(1, chips):
        own = own + turn(chip_sums[rel], 2 * rel)
    fresh = momentum_decay * mom_near + factor[0, 0] * grad_near.astype(F32)
    own, fresh = lax.optimization_barrier((own, fresh))
    other = turn(own, 1)

    full_rows = sent_rows(tail)
    piece = full_rows // 2
    mine, theirs = pl.pallas_call(
        functools.partial(newton_kernel, owners, width),
        in_specs=[near_by] * 2,
        out_specs=[near_by] * 2,
        out_shape=[jax.ShapeDtypeStruct((piece, LANES), BF16)] * 2,
        scratch_shapes=[
            pltpu.VMEM((packed, LANES), F32),
            pltpu.VMEM((packed, LANES), F32),
            pltpu.VMEM((full_rows, LANES), BF16),
        ],
        compiler_params=params(),
        name="newton",
    )(own, other)

    arriving = {}
    for k in range(1, chips):
        arriving[k] = turn(mine, 2 * k)
    update = means = None
    flops = 4 * width * width * rows
    for rel in range(chips):
        group = (rel,)
        last = rel == chips - 1
        operands = [assignment, start]
        if group[0]:
            near = arriving[rel]
            operands += [near, turn(near, 1)]
        else:
            operands += [mine, theirs]
        in_specs = [pl.BlockSpec(memory_space=pltpu.SMEM)] + [near_by] * (len(operands) - 1)
        aliases = {}
        if group[0]:
            aliases = {len(operands) + 1: 0}
            operands += [means, update]
            in_specs += [near_by, pl.BlockSpec(memory_space=pl.ANY)]
        call = pl.pallas_call(
            functools.partial(update_kernel, math.sqrt(owners * rows), width, group, last),
            in_specs=in_specs,
            out_specs=[
                pl.BlockSpec(memory_space=pl.ANY),
                pl.BlockSpec(memory_space=pl.ANY) if last else near_by,
            ],
            out_shape=[
                jax.ShapeDtypeStruct((layers, width, rows), BF16),
                jax.ShapeDtypeStruct((1, MAXOWN) if last else (8, LANES), F32),
            ],
            scratch_shapes=[
                pltpu.VMEM((len(group), full_rows, LANES), BF16),
                pltpu.VMEM((len(group), width, rows), BF16),
                pltpu.SemaphoreType.DMA((len(group),)),
            ]
            + [pltpu.VMEM((1, MAXOWN), F32), pltpu.SemaphoreType.DMA] * last,
            input_output_aliases=aliases,
            compiler_params=params(),
            cost_estimate=cost(
                len(group) * flops, len(group) * (4 * width * rows + 4 * piece * LANES)
            ),
            name="update",
        )
        update, means = call(*operands)
    return (jnp.swapaxes(fresh, 1, 2)[None], jnp.swapaxes(update, 1, 2)[None], means)


def solution(mesh):
    in_specs = (P("section", None, "dp", None), P("section", None, "dp", None), P("section", None))
    out_specs = (P("section", None, "dp", None), P("section", None, "dp", None), P("section", "dp"))
    return jax.shard_map(step, mesh=mesh, in_specs=in_specs, out_specs=out_specs, check_vma=False)
```

```python
import functools
import math

import jax
import jax.numpy as jnp
from jax import lax
from jax.experimental import pallas as pl
from jax.experimental.pallas import tpu as pltpu
from jax.sharding import PartitionSpec as P


MAXOWN = 2
NS_STEPS = 5
LANES = 128

momentum_decay = 0.95
clip_rms = 0.5
newton_coeffs = (3.4445, -4.775, 2.0315)

F32 = jnp.float32
BF16 = jnp.bfloat16


VMEM_BYTES = 12 * 2**20


def params():
    return pltpu.CompilerParams(vmem_limit_bytes=VMEM_BYTES)


def cost(flops, bytes_accessed):
    return pl.CostEstimate(flops=flops, bytes_accessed=bytes_accessed, transcendentals=0)


def over(count, visit):
    if count <= 8:
        for i in range(count):
            visit(i)
    else:
        pl.loop(0, count)(visit)


def total_of(values):
    return jnp.sum(jnp.sum(values, axis=0, keepdims=True), axis=1, keepdims=True)


def sums_kernel(layers, grad_in, mom_in, out_ref, grad_ref, mom_ref, acc, sems):
    def copies(layer):
        return (
            pltpu.make_async_copy(grad_in.at[layer], grad_ref.at[layer], sems.at[layer, 0]),
            pltpu.make_async_copy(mom_in.at[layer], mom_ref.at[layer], sems.at[layer, 1]),
        )

    def begin(layer):
        for copy in copies(layer):
            copy.start()

    def visit(layer):
        for copy in copies(layer):
            copy.wait()
        grads = grad_ref[layer].astype(F32)
        moms = mom_ref[layer]
        for i, prod in enumerate((grads * grads, grads * moms, moms * moms)):
            acc[pl.ds(3 * layer + i, 1), :] = jnp.sum(prod, axis=0, keepdims=True)

    acc[...] = jnp.zeros_like(acc)
    over(layers, begin)
    over(layers, visit)
    column = jnp.sum(acc[...], axis=1, keepdims=True)
    shape = (acc.shape[0], out_ref.shape[1])
    hit = lax.broadcasted_iota(jnp.int32, shape, 0) == lax.broadcasted_iota(jnp.int32, shape, 1)
    line = jnp.sum(jnp.where(hit, column, 0.0), axis=0, keepdims=True)
    out_ref[...] = jnp.broadcast_to(line, out_ref.shape)


def pair_nt(left, right):
    return lax.dot_general(left, right, (((1,), (1,)), ((), ())), preferred_element_type=F32)


def start_kernel(
    layers, entries, owners, sums_ref, grad_ref, mom_ref, start_ref, keep_ref, send_ref, fac_ref, pack
):
    place = lax.axis_index("dp")
    chip, core, section = place >> 1, place & 1, lax.axis_index("section")
    lane = lax.broadcasted_iota(jnp.int32, (1, sums_ref.shape[1]), 1)
    every = jnp.sum(sums_ref[...], axis=0, keepdims=True)
    mine = sums_ref[pl.ds(pl.multiple_of(section * owners, 8), owners), :]
    mine = jnp.sum(mine, axis=0, keepdims=True)
    kind = lax.rem(lane, 3)
    total = jnp.sum(jnp.where(kind == 0, every, 0.0), axis=1, keepdims=True)
    factor = clip_rms / jnp.sqrt(total / entries + 1e-06)
    fac_ref[...] = jnp.broadcast_to(factor, fac_ref.shape)
    on_grad = factor * (1.0 + momentum_decay)
    on_mom = momentum_decay * momentum_decay
    cross = 2.0 * (on_grad * on_mom)
    known = mine * jnp.where(
        kind == 0, on_grad * on_grad, jnp.where(kind == 1, cross, on_mom * on_mom)
    )

    def visit(layer):
        here = (lane >= 3 * layer) & (lane < 3 * layer + 3)
        guess = jnp.maximum(jnp.sum(jnp.where(here, known, 0.0), axis=1, keepdims=True), 0.0)
        scale = 1.0 / (jnp.sqrt(guess) + 1e-07)
        scaled = factor * grad_ref[layer].astype(F32)
        fresh = momentum_decay * mom_ref[layer] + scaled
        nesterov = (scaled + momentum_decay * fresh).astype(BF16).astype(F32)
        squares = total_of(nesterov * nesterov)
        start = (nesterov * scale).astype(BF16)
        start_ref[layer] = start
        width = start.shape[0]
        tail = width - 2 * LANES
        a, b = LANES, 2 * LANES
        gram = pair_nt(start[0:b], start[0:b])
        edge = pair_nt(start[b:], start)
        hold = pack.at[lax.rem(layer, 2)]
        down, across = grid_of(LANES)
        t11 = gram[a:b, a:b]
        hold[0:a, :] = jnp.where(down >= across, gram[0:a, 0:a], t11)
        hold[a:b, :] = gram[0:a, a:b]
        hold[b : b + tail, :] = edge[:, 0:a]
        hold[b + tail : b + 2 * tail, :] = edge[:, a:b]
        at = b + 2 * tail
        small = tail * tail // LANES
        lay_corner(hold, at, edge[:, b:])
        diagonal = jnp.sum(jnp.where(down == across, t11, 0.0), axis=0, keepdims=True)
        row, spot = lax.broadcasted_iota(jnp.int32, (8, LANES), 0), lax.broadcasted_iota(jnp.int32, (8, LANES), 1)
        extra = jnp.where(spot == 0, squares, jnp.where(spot == 1, guess, 0.0))
        hold[at + small :, :] = jnp.where(row == 0, diagonal, extra)
        half = pack.shape[1] // 2
        keep_ref[layer ^ chip] = hold[pl.ds(pl.multiple_of(core * half, 8), half), :]
        send_ref[layer ^ chip] = hold[pl.ds(pl.multiple_of((1 - core) * half, 8), half), :]

    over(layers, visit)


def grid_of(size):
    return lax.broadcasted_iota(jnp.int32, (size, size), 0), lax.broadcasted_iota(jnp.int32, (size, size), 1)


def packed_rows(tail):
    return 2 * LANES + 2 * tail + tail * tail // LANES + 8


def lay_corner(hold, at, block):
    tail = block.shape[1]
    small = tail * tail // LANES
    for i in range(LANES // tail):
        hold[at : at + small, i * tail : (i + 1) * tail] = block[i * small : (i + 1) * small]


def read_corner(block, tail):
    return jnp.concatenate([block[:, i * tail : (i + 1) * tail] for i in range(LANES // tail)], axis=0)


def half_of(ref, core, half, align=8):
    return ref.at[pl.ds(pl.multiple_of(core * half, align), half)]


def sent_rows(tail):
    return -(-3 * packed_rows(tail) // 32) * 32


def split(value):
    high = value.astype(BF16)
    return high, (value - high.astype(F32)).astype(BF16)


def dot(left, right):
    return jnp.dot(left, right, preferred_element_type=F32)


def wide_left(left, right):
    high, low = split(left)
    b = 2 * LANES
    ends = jnp.concatenate([high[:, b:], low[:, b:]], axis=1)
    rest = jnp.concatenate([right[b:], right[b:]], axis=0)
    return dot(high[:, :b], right[:b]) + dot(low[:, :b], right[:b]) + dot(ends, rest)


def wide_right(left, right):
    high, low = split(right)
    b = 2 * LANES
    ends = jnp.concatenate([left[:, b:], left[:, b:]], axis=1)
    rest = jnp.concatenate([high[b:], low[b:]], axis=0)
    return dot(left[:, :b], high[:b]) + dot(left[:, :b], low[:b]) + dot(ends, rest)


def newton_kernel(owners, width, own_ref, other_ref, mine_ref, theirs_ref, pack, skew, full):
    core = lax.axis_index("dp") & 1
    half = own_ref.shape[0]
    pack[pl.ds(pl.multiple_of(core * half, 8), half), :] = own_ref[...]
    pack[pl.ds(pl.multiple_of((1 - core) * half, 8), half), :] = other_ref[...]
    tail = width - 2 * LANES
    a, b = LANES, 2 * LANES
    merged, t01 = pack[0:a, :], pack[a:b, :]
    t20, t21 = pack[b : b + tail, :], pack[b + tail : b + 2 * tail, :]
    at = b + 2 * tail
    small = tail * tail // LANES
    t22 = read_corner(pack[at : at + small, :], tail)
    extra = pack[at + small :, :]
    down, across = grid_of(LANES)
    flipped = merged.T
    t00 = jnp.where(down >= across, merged, flipped)
    t11 = jnp.where(down == across, extra[0:1, :], jnp.where(down < across, merged, flipped))
    squares = extra[1:2, 0:1]
    guess = extra[1:2, 1:2] * (1.0 / owners)
    ratio = (jnp.sqrt(guess) + 1e-07) / (jnp.sqrt(squares) + 1e-07)
    gram = jnp.concatenate(
        [
            jnp.concatenate([t00, t01, t20.T], axis=1),
            jnp.concatenate([t01.T, t11, t21.T], axis=1),
            jnp.concatenate([t20, t21, t22], axis=1),
        ],
        axis=0,
    )
    gram = gram * (ratio * ratio)
    ca, cb, cc = newton_coeffs
    rows = lax.broadcasted_iota(jnp.int32, (width, width), 0)
    cols = lax.broadcasted_iota(jnp.int32, (width, width), 1)
    eye = rows == cols
    prod = None
    mean_sq = None
    for step in range(NS_STEPS):
        rounded = gram.astype(BF16)
        mix = (cb * rounded.astype(F32) + cc * dot(rounded, rounded)).astype(BF16)
        if step < NS_STEPS - 1:
            turned = ca * gram + wide_right(mix, gram)
            gram = ca * turned + wide_left(turned, mix)
        else:
            inner = dot(mix, mix) + (2.0 * ca) * mix.astype(F32) + jnp.where(eye, ca * ca, 0.0)
            mean_sq = total_of(gram * inner) * (1.0 / width)
        if step == 0:
            before = mix
        elif step == 1:
            both = ca * (before.astype(F32) + mix.astype(F32)) + dot(mix, before)
            prod = both + jnp.where(eye, ca * ca, 0.0)
        else:
            prod = ca * prod + wide_right(mix, prod)
    prod = ratio * prod
    p00, p11 = prod[0:a, 0:a], prod[a:b, a:b]
    back00, back11 = p00.T, p11.T
    p01, back10 = prod[0:a, a:b], prod[a:b, 0:a].T
    p2, back2 = prod[b:, 0:b], prod[0:b, b:].T
    p22 = prod[b:, b:]
    lower = down >= across
    for ref, sign in ((pack, 1.0), (skew, -1.0)):
        ref[0:a, :] = 0.5 * jnp.where(lower, p00 + sign * back00, p11 + sign * back11)
        ref[a:b, :] = 0.5 * (p01 + sign * back10)
        edge = 0.5 * (p2 + sign * back2)
        ref[b : b + tail, :] = edge[:, 0:a]
        ref[b + tail : at, :] = edge[:, a:b]
        lay_corner(ref, at, p22 if ref is pack else jnp.zeros_like(p22))
    diagonal = jnp.sum(jnp.where(down == across, p11, 0.0), axis=0, keepdims=True)
    first = lax.broadcasted_iota(jnp.int32, (8, LANES), 0) == 0
    pack[at + small :, :] = jnp.where(first, diagonal, mean_sq)
    skew[at + small :, :] = jnp.zeros((8, LANES), F32)
    rows = pack.shape[0]
    high, low = split(pack[...])
    full[0:rows, :] = high
    full[rows : 2 * rows, :] = low
    full[2 * rows : 3 * rows, :] = skew[...].astype(BF16)
    if full.shape[0] > 3 * rows:
        full[3 * rows :, :] = jnp.zeros((full.shape[0] - 3 * rows, LANES), BF16)
    half = mine_ref.shape[0]
    mine_ref[...] = half_of(full, core, half, 16)[...]
    theirs_ref[...] = half_of(full, 1 - core, half, 16)[...]


def update_kernel(scale, width, rel, last, *refs):
    if rel == 0:
        start_ref, mine_ref, other_ref, owner_ref, out_ref, means_out, full, values, sems = refs
    elif last:
        start_ref, mine_ref, other_ref, means_ref, _, out_ref, slot_out, full, values, sems, slot_ref = refs
    else:
        start_ref, mine_ref, other_ref, means_ref, _, out_ref, means_out, full, values, sems = refs
    place = lax.axis_index("dp")
    chip, core = place >> 1, place & 1
    layer = chip ^ rel
    tail = width - 2 * LANES
    b = 2 * LANES
    half = mine_ref.shape[0]
    half_of(full, core, half, 16)[...] = mine_ref[...]
    half_of(full, 1 - core, half, 16)[...] = other_ref[...]
    size = packed_rows(tail)
    even = full[0:size, :].astype(F32) + full[size : 2 * size, :].astype(F32)
    odd = full[2 * size : 3 * size, :].astype(F32)
    plus, minus = even + odd, even - odd
    at = b + 2 * tail
    small = tail * tail // LANES
    extra = even[at + small :]
    start = start_ref[layer]
    rest = jnp.concatenate([start[b:], start[b:]], axis=0)
    down, across = grid_of(LANES)
    turned = minus[0:LANES].T
    p00 = jnp.where(down >= across, plus[0:LANES], turned)
    p11 = jnp.where(down == across, extra[0:1], jnp.where(down < across, plus[0:LANES], turned))
    p10 = minus[LANES:b].T
    strips = (
        (p00, plus[LANES:b], minus[b : b + tail].T),
        (p10, p11, minus[b + tail : at].T),
        (plus[b : b + tail], plus[b + tail : at], read_corner(even[at : at + small], tail)),
    )
    copies = []
    first = 0
    for i, strip in enumerate(strips):
        high, low = split(jnp.concatenate(strip[:2], axis=1))
        ends = jnp.concatenate(split(strip[2]), axis=1)
        value = dot(high, start[:b]) + dot(low, start[:b]) + dot(ends, rest)
        strip_rows = pl.ds(first, value.shape[0])
        values[strip_rows, :] = (value * scale).astype(BF16)
        copies.append(
            pltpu.make_async_copy(values.at[strip_rows], out_ref.at[layer, strip_rows], sems.at[i])
        )
        copies[-1].start()
        first += value.shape[0]
    row = lax.broadcasted_iota(jnp.int32, (8, LANES), 0)
    lane = lax.broadcasted_iota(jnp.int32, (8, LANES), 1)
    means = jnp.where((row == 0) & (lane == layer), extra[1:2], 0.0)
    if rel:
        means = means + means_ref[...]
    else:
        for slot in range(MAXOWN):

            def visit(j, carry):
                seen, at = carry
                hit = owner_ref[0, j] == place
                at = jnp.where(hit & (seen == slot), j, at)
                return seen + jnp.where(hit, 1, 0), at

            _, at = lax.fori_loop(0, owner_ref.shape[1], visit, (jnp.int32(0), jnp.int32(-1)))
            means = jnp.where((row == 1 + slot) & (lane == at), 1.0, means)
    if last:
        chosen = jnp.where(means > 0.0, means[0:1], 0.0)
        spots = lax.broadcasted_iota(jnp.int32, slot_ref.shape, 1)
        line = jnp.zeros(slot_ref.shape, F32)
        for slot in range(MAXOWN):
            value = jnp.sum(chosen[1 + slot : 2 + slot], axis=1, keepdims=True)
            line = jnp.where(spots == slot, value, line)
        slot_ref[...] = line
        copies.append(pltpu.make_async_copy(slot_ref, slot_out, sems.at[len(strips)]))
        copies[-1].start()
    else:
        means_out[...] = means
    for copy in copies:
        copy.wait()


def step(momentum, gradient, assignment):
    _, layers, rows, width = momentum.shape
    owners = lax.axis_size("dp")
    sections = lax.axis_size("section")
    chips = owners // 2
    tail = width - 2 * LANES
    assert chips == layers and chips & (chips - 1) == 0 and LANES % tail == 0 and 3 * layers <= LANES
    everyone = sections * owners
    entries = everyone * layers * rows * width
    mom = jnp.swapaxes(momentum[0], 1, 2)
    grad = jnp.swapaxes(gradient[0], 1, 2)
    anywhere = pl.BlockSpec(memory_space=pl.ANY)
    near_by = pl.BlockSpec(memory_space=pltpu.VMEM)
    sums, grad_near, mom_near = pl.pallas_call(
        functools.partial(sums_kernel, layers),
        in_specs=[anywhere, anywhere],
        out_specs=[near_by] * 3,
        out_shape=[
            jax.ShapeDtypeStruct((everyone, LANES), F32),
            jax.ShapeDtypeStruct(grad.shape, BF16),
            jax.ShapeDtypeStruct(mom.shape, F32),
        ],
        scratch_shapes=[
            pltpu.VMEM((-(-3 * layers // 8) * 8, rows), F32),
            pltpu.SemaphoreType.DMA((layers, 2)),
        ],
        compiler_params=params(),
        name="sums",
    )(pltpu.with_memory_space_constraint(grad, pltpu.HBM), pltpu.with_memory_space_constraint(mom, pltpu.HBM))
    sums = lax.all_to_all(sums, ("section", "dp"), 0, 0, tiled=True)

    packed = packed_rows(tail)
    half = packed // 2
    start, keep, send, factor = pl.pallas_call(
        functools.partial(start_kernel, layers, entries, owners),
        in_specs=[near_by] * 3,
        out_specs=[near_by] * 4,
        out_shape=[
            jax.ShapeDtypeStruct((layers, width, rows), BF16),
            jax.ShapeDtypeStruct((layers, half, LANES), F32),
            jax.ShapeDtypeStruct((layers, half, LANES), F32),
            jax.ShapeDtypeStruct((8, LANES), F32),
        ],
        scratch_shapes=[pltpu.VMEM((2, packed, LANES), F32)],
        compiler_params=params(),
        name="start",
    )(sums, grad_near, mom_near)

    def turn(value, by):
        return lax.ppermute(value, "dp", [(i, i ^ by) for i in range(owners)])

    chip_sums = keep + turn(send, 1)
    own = chip_sums[0]
    for rel in range(1, chips):
        own = own + turn(chip_sums[rel], 2 * rel)
    fresh = momentum_decay * mom_near + factor[0, 0] * grad_near.astype(F32)
    own, fresh = lax.optimization_barrier((own, fresh))
    other = turn(own, 1)

    full_rows = sent_rows(tail)
    piece = full_rows // 2
    mine, theirs = pl.pallas_call(
        functools.partial(newton_kernel, owners, width),
        in_specs=[near_by] * 2,
        out_specs=[near_by] * 2,
        out_shape=[jax.ShapeDtypeStruct((piece, LANES), BF16)] * 2,
        scratch_shapes=[
            pltpu.VMEM((packed, LANES), F32),
            pltpu.VMEM((packed, LANES), F32),
            pltpu.VMEM((full_rows, LANES), BF16),
        ],
        compiler_params=params(),
        name="newton",
    )(own, other)

    arriving = {}
    for k in range(1, chips):
        arriving[k] = turn(mine, 2 * k)
    update = means = None
    flops = 4 * width * width * rows
    for rel in range(chips):
        last = rel == chips - 1
        operands, in_specs = [start], [near_by] * 3
        aliases = {}
        if rel:
            near = arriving[rel]
            operands += [near, turn(near, 1)]
            operands += [means, update]
            in_specs += [near_by, pl.BlockSpec(memory_space=pl.ANY)]
            aliases = {4: 0}
        else:
            operands += [mine, theirs, assignment]
            in_specs.append(pl.BlockSpec(memory_space=pltpu.SMEM))
        call = pl.pallas_call(
            functools.partial(update_kernel, math.sqrt(owners * rows), width, rel, last),
            in_specs=in_specs,
            out_specs=[
                pl.BlockSpec(memory_space=pl.ANY),
                pl.BlockSpec(memory_space=pl.ANY) if last else near_by,
            ],
            out_shape=[
                jax.ShapeDtypeStruct((layers, width, rows), BF16),
                jax.ShapeDtypeStruct((1, MAXOWN) if last else (8, LANES), F32),
            ],
            scratch_shapes=[
                pltpu.VMEM((full_rows, LANES), BF16),
                pltpu.VMEM((width, rows), BF16),
                pltpu.SemaphoreType.DMA((4,)),
            ]
            + [pltpu.VMEM((1, MAXOWN), F32)] * last,
            input_output_aliases=aliases,
            compiler_params=params(),
            cost_estimate=cost(flops, 4 * width * rows + 4 * piece * LANES),
            name="update",
        )
        update, means = call(*operands)
    return (jnp.swapaxes(fresh, 1, 2)[None], jnp.swapaxes(update, 1, 2)[None], means)


def solution(mesh):
    in_specs = (P("section", None, "dp", None), P("section", None, "dp", None), P("section", None))
    out_specs = (P("section", None, "dp", None), P("section", None, "dp", None), P("section", "dp"))
    return jax.shard_map(step, mesh=mesh, in_specs=in_specs, out_specs=out_specs, check_vma=False)
```

```python
import functools
import math

import jax
import jax.numpy as jnp
from jax import lax
from jax.experimental import pallas as pl
from jax.experimental.pallas import tpu as pltpu
from jax.sharding import PartitionSpec as P


MAXOWN = 2
STRIP = 32
NS_STEPS = 5
LANES = 128

momentum_decay = 0.95
clip_rms = 0.5
newton_coeffs = (3.4445, -4.775, 2.0315)

F32 = jnp.float32
BF16 = jnp.bfloat16


VMEM_BYTES = 12 * 2**20


def params():
    return pltpu.CompilerParams(vmem_limit_bytes=VMEM_BYTES)


def cost(flops, bytes_accessed):
    return pl.CostEstimate(flops=flops, bytes_accessed=bytes_accessed, transcendentals=0)


def over(count, visit):
    if count <= 8:
        for i in range(count):
            visit(i)
    else:
        pl.loop(0, count)(visit)


def total_of(values):
    return jnp.sum(jnp.sum(values, axis=0, keepdims=True), axis=1, keepdims=True)


def sums_kernel(layers, grad_in, mom_in, out_ref, grad_ref, mom_ref, acc, sems):
    def copies(layer):
        return (
            pltpu.make_async_copy(grad_in.at[layer], grad_ref.at[layer], sems.at[layer, 0]),
            pltpu.make_async_copy(mom_in.at[layer], mom_ref.at[layer], sems.at[layer, 1]),
        )

    def begin(layer):
        for copy in copies(layer):
            copy.start()

    def visit(layer):
        for copy in copies(layer):
            copy.wait()
        kept = [0.0, 0.0, 0.0]
        for first in range(0, grad_ref.shape[1], STRIP):
            grads = grad_ref[layer, first : first + STRIP].astype(F32)
            moms = mom_ref[layer, first : first + STRIP]
            for i, prod in enumerate((grads * grads, grads * moms, moms * moms)):
                kept[i] = kept[i] + (prod[: STRIP // 2] + prod[STRIP // 2 :])
        for i in range(3):
            acc[pl.ds(3 * layer + i, 1), :] = jnp.sum(kept[i], axis=0, keepdims=True)

    acc[...] = jnp.zeros_like(acc)
    over(layers, begin)
    over(layers, visit)
    column = jnp.sum(acc[...], axis=1, keepdims=True)
    shape = (acc.shape[0], out_ref.shape[1])
    hit = lax.broadcasted_iota(jnp.int32, shape, 0) == lax.broadcasted_iota(jnp.int32, shape, 1)
    line = jnp.sum(jnp.where(hit, column, 0.0), axis=0, keepdims=True)
    out_ref[...] = jnp.broadcast_to(line, out_ref.shape)


def pair_nt(left, right):
    return lax.dot_general(left, right, (((1,), (1,)), ((), ())), preferred_element_type=F32)


def start_kernel(
    layers, entries, owners, sums_ref, grad_ref, mom_ref, start_ref, keep_ref, send_ref, fac_ref, pack
):
    place = lax.axis_index("dp")
    chip, core, section = place >> 1, place & 1, lax.axis_index("section")
    lane = lax.broadcasted_iota(jnp.int32, (1, sums_ref.shape[1]), 1)
    every = jnp.sum(sums_ref[...], axis=0, keepdims=True)
    mine = sums_ref[pl.ds(pl.multiple_of(section * owners, 8), owners), :]
    mine = jnp.sum(mine, axis=0, keepdims=True)
    kind = lax.rem(lane, 3)
    total = jnp.sum(jnp.where(kind == 0, every, 0.0), axis=1, keepdims=True)
    factor = clip_rms / jnp.sqrt(total / entries + 1e-06)
    fac_ref[...] = jnp.broadcast_to(factor, fac_ref.shape)
    on_grad = factor * (1.0 + momentum_decay)
    on_mom = momentum_decay * momentum_decay
    cross = 2.0 * (on_grad * on_mom)
    known = mine * jnp.where(
        kind == 0, on_grad * on_grad, jnp.where(kind == 1, cross, on_mom * on_mom)
    )

    def visit(layer):
        here = (lane >= 3 * layer) & (lane < 3 * layer + 3)
        guess = jnp.maximum(jnp.sum(jnp.where(here, known, 0.0), axis=1, keepdims=True), 0.0)
        scale = 1.0 / (jnp.sqrt(guess) + 1e-07)
        width = grad_ref.shape[1]
        kept = 0.0
        for first in range(0, width, STRIP):
            scaled = factor * grad_ref[layer, first : first + STRIP].astype(F32)
            fresh = momentum_decay * mom_ref[layer, first : first + STRIP] + scaled
            nesterov = (scaled + momentum_decay * fresh).astype(BF16).astype(F32)
            start_ref[layer, first : first + STRIP, :] = (nesterov * scale).astype(BF16)
            square = nesterov * nesterov
            kept = kept + (square[: STRIP // 2] + square[STRIP // 2 :])
        squares = total_of(kept)
        start = start_ref[layer]
        tail = width - 2 * LANES
        a, b = LANES, 2 * LANES
        gram = pair_nt(start[0:b], start[0:b])
        edge = pair_nt(start[b:], start)
        hold = pack.at[lax.rem(layer, 2)]
        down, across = grid_of(LANES)
        t11 = gram[a:b, a:b]
        hold[0:a, :] = jnp.where(down >= across, gram[0:a, 0:a], t11)
        hold[a:b, :] = gram[0:a, a:b]
        hold[b : b + tail, :] = edge[:, 0:a]
        hold[b + tail : b + 2 * tail, :] = edge[:, a:b]
        at = b + 2 * tail
        small = tail * tail // LANES
        lay_corner(hold, at, edge[:, b:])
        diagonal = jnp.sum(jnp.where(down == across, t11, 0.0), axis=0, keepdims=True)
        row, spot = lax.broadcasted_iota(jnp.int32, (8, LANES), 0), lax.broadcasted_iota(jnp.int32, (8, LANES), 1)
        extra = jnp.where(spot == 0, squares, jnp.where(spot == 1, guess, 0.0))
        hold[at + small :, :] = jnp.where(row == 0, diagonal, extra)
        half = pack.shape[1] // 2
        keep_ref[layer ^ chip] = hold[pl.ds(pl.multiple_of(core * half, 8), half), :]
        send_ref[layer ^ chip] = hold[pl.ds(pl.multiple_of((1 - core) * half, 8), half), :]

    over(layers, visit)


def grid_of(size):
    return lax.broadcasted_iota(jnp.int32, (size, size), 0), lax.broadcasted_iota(jnp.int32, (size, size), 1)


def packed_rows(tail):
    return 2 * LANES + 2 * tail + tail * tail // LANES + 8


def lay_corner(hold, at, block):
    tail = block.shape[1]
    small = tail * tail // LANES
    for i in range(LANES // tail):
        hold[at : at + small, i * tail : (i + 1) * tail] = block[i * small : (i + 1) * small]


def read_corner(block, tail):
    return jnp.concatenate([block[:, i * tail : (i + 1) * tail] for i in range(LANES // tail)], axis=0)


def half_of(ref, core, half, align=8):
    return ref.at[pl.ds(pl.multiple_of(core * half, align), half)]


def sent_rows(tail):
    return -(-3 * packed_rows(tail) // 32) * 32


def split(value):
    high = value.astype(BF16)
    return high, (value - high.astype(F32)).astype(BF16)


def dot(left, right):
    return jnp.dot(left, right, preferred_element_type=F32)


def wide_left(left, right):
    high, low = split(left)
    b = 2 * LANES
    ends = jnp.concatenate([high[:, b:], low[:, b:]], axis=1)
    rest = jnp.concatenate([right[b:], right[b:]], axis=0)
    return dot(high[:, :b], right[:b]) + dot(low[:, :b], right[:b]) + dot(ends, rest)


def wide_right(left, right):
    high, low = split(right)
    b = 2 * LANES
    ends = jnp.concatenate([left[:, b:], left[:, b:]], axis=1)
    rest = jnp.concatenate([high[b:], low[b:]], axis=0)
    return dot(left[:, :b], high[:b]) + dot(left[:, :b], low[:b]) + dot(ends, rest)


def newton_kernel(owners, width, own_ref, other_ref, mine_ref, theirs_ref, pack, skew, full):
    core = lax.axis_index("dp") & 1
    half = own_ref.shape[0]
    pack[pl.ds(pl.multiple_of(core * half, 8), half), :] = own_ref[...]
    pack[pl.ds(pl.multiple_of((1 - core) * half, 8), half), :] = other_ref[...]
    tail = width - 2 * LANES
    a, b = LANES, 2 * LANES
    merged, t01 = pack[0:a, :], pack[a:b, :]
    t20, t21 = pack[b : b + tail, :], pack[b + tail : b + 2 * tail, :]
    at = b + 2 * tail
    small = tail * tail // LANES
    t22 = read_corner(pack[at : at + small, :], tail)
    extra = pack[at + small :, :]
    down, across = grid_of(LANES)
    flipped = merged.T
    t00 = jnp.where(down >= across, merged, flipped)
    t11 = jnp.where(down == across, extra[0:1, :], jnp.where(down < across, merged, flipped))
    squares = extra[1:2, 0:1]
    guess = extra[1:2, 1:2] * (1.0 / owners)
    ratio = (jnp.sqrt(guess) + 1e-07) / (jnp.sqrt(squares) + 1e-07)
    gram = jnp.concatenate(
        [
            jnp.concatenate([t00, t01, t20.T], axis=1),
            jnp.concatenate([t01.T, t11, t21.T], axis=1),
            jnp.concatenate([t20, t21, t22], axis=1),
        ],
        axis=0,
    )
    gram = gram * (ratio * ratio)
    ca, cb, cc = newton_coeffs
    rows = lax.broadcasted_iota(jnp.int32, (width, width), 0)
    cols = lax.broadcasted_iota(jnp.int32, (width, width), 1)
    eye = rows == cols
    prod = None
    mean_sq = None
    for step in range(NS_STEPS):
        rounded = gram.astype(BF16)
        mix = (cb * rounded.astype(F32) + cc * dot(rounded, rounded)).astype(BF16)
        if step < NS_STEPS - 1:
            turned = ca * gram + wide_right(mix, gram)
            gram = ca * turned + wide_left(turned, mix)
        else:
            inner = dot(mix, mix) + (2.0 * ca) * mix.astype(F32) + jnp.where(eye, ca * ca, 0.0)
            mean_sq = total_of(gram * inner) * (1.0 / width)
        if step == 0:
            before = mix
        elif step == 1:
            both = ca * (before.astype(F32) + mix.astype(F32)) + dot(mix, before)
            prod = both + jnp.where(eye, ca * ca, 0.0)
        else:
            prod = ca * prod + wide_right(mix, prod)
    prod = ratio * prod
    p00, p11 = prod[0:a, 0:a], prod[a:b, a:b]
    back00, back11 = p00.T, p11.T
    p01, back10 = prod[0:a, a:b], prod[a:b, 0:a].T
    p2, back2 = prod[b:, 0:b], prod[0:b, b:].T
    p22 = prod[b:, b:]
    lower = down >= across
    for ref, sign in ((pack, 1.0), (skew, -1.0)):
        ref[0:a, :] = 0.5 * jnp.where(lower, p00 + sign * back00, p11 + sign * back11)
        ref[a:b, :] = 0.5 * (p01 + sign * back10)
        edge = 0.5 * (p2 + sign * back2)
        ref[b : b + tail, :] = edge[:, 0:a]
        ref[b + tail : at, :] = edge[:, a:b]
        lay_corner(ref, at, p22 if ref is pack else jnp.zeros_like(p22))
    diagonal = jnp.sum(jnp.where(down == across, p11, 0.0), axis=0, keepdims=True)
    first = lax.broadcasted_iota(jnp.int32, (8, LANES), 0) == 0
    pack[at + small :, :] = jnp.where(first, diagonal, mean_sq)
    skew[at + small :, :] = jnp.zeros((8, LANES), F32)
    rows = pack.shape[0]
    high, low = split(pack[...])
    full[0:rows, :] = high
    full[rows : 2 * rows, :] = low
    full[2 * rows : 3 * rows, :] = skew[...].astype(BF16)
    if full.shape[0] > 3 * rows:
        full[3 * rows :, :] = jnp.zeros((full.shape[0] - 3 * rows, LANES), BF16)
    half = mine_ref.shape[0]
    mine_ref[...] = half_of(full, core, half, 16)[...]
    theirs_ref[...] = half_of(full, 1 - core, half, 16)[...]


def update_kernel(scale, width, rel, last, *refs):
    if rel == 0:
        start_ref, mine_ref, other_ref, owner_ref, out_ref, means_out, full, values, sems = refs
    elif last:
        start_ref, mine_ref, other_ref, means_ref, _, out_ref, slot_out, full, values, sems, slot_ref = refs
    else:
        start_ref, mine_ref, other_ref, means_ref, _, out_ref, means_out, full, values, sems = refs
    place = lax.axis_index("dp")
    chip, core = place >> 1, place & 1
    layer = chip ^ rel
    tail = width - 2 * LANES
    b = 2 * LANES
    half = mine_ref.shape[0]
    half_of(full, core, half, 16)[...] = mine_ref[...]
    half_of(full, 1 - core, half, 16)[...] = other_ref[...]
    size = packed_rows(tail)
    even = full[0:size, :].astype(F32) + full[size : 2 * size, :].astype(F32)
    odd = full[2 * size : 3 * size, :].astype(F32)
    plus, minus = even + odd, even - odd
    at = b + 2 * tail
    small = tail * tail // LANES
    extra = even[at + small :]
    start = start_ref[layer]
    rest = jnp.concatenate([start[b:], start[b:]], axis=0)
    down, across = grid_of(LANES)
    turned = minus[0:LANES].T
    p00 = jnp.where(down >= across, plus[0:LANES], turned)
    p11 = jnp.where(down == across, extra[0:1], jnp.where(down < across, plus[0:LANES], turned))
    p10 = minus[LANES:b].T
    strips = (
        (p00, plus[LANES:b], minus[b : b + tail].T),
        (p10, p11, minus[b + tail : at].T),
        (plus[b : b + tail], plus[b + tail : at], read_corner(even[at : at + small], tail)),
    )
    copies = []
    first = 0
    for i, strip in enumerate(strips):
        high, low = split(jnp.concatenate(strip[:2], axis=1))
        ends = jnp.concatenate(split(strip[2]), axis=1)
        value = dot(high, start[:b]) + dot(low, start[:b]) + dot(ends, rest)
        strip_rows = pl.ds(first, value.shape[0])
        values[strip_rows, :] = (value * scale).astype(BF16)
        copies.append(
            pltpu.make_async_copy(values.at[strip_rows], out_ref.at[layer, strip_rows], sems.at[i])
        )
        copies[-1].start()
        first += value.shape[0]
    row = lax.broadcasted_iota(jnp.int32, (8, LANES), 0)
    lane = lax.broadcasted_iota(jnp.int32, (8, LANES), 1)
    means = jnp.where((row == 0) & (lane == layer), extra[1:2], 0.0)
    if rel:
        means = means + means_ref[...]
    else:
        for slot in range(MAXOWN):

            def visit(j, carry):
                seen, at = carry
                hit = owner_ref[0, j] == place
                at = jnp.where(hit & (seen == slot), j, at)
                return seen + jnp.where(hit, 1, 0), at

            _, at = lax.fori_loop(0, owner_ref.shape[1], visit, (jnp.int32(0), jnp.int32(-1)))
            means = jnp.where((row == 1 + slot) & (lane == at), 1.0, means)
    if last:
        chosen = jnp.where(means > 0.0, means[0:1], 0.0)
        spots = lax.broadcasted_iota(jnp.int32, slot_ref.shape, 1)
        line = jnp.zeros(slot_ref.shape, F32)
        for slot in range(MAXOWN):
            value = jnp.sum(chosen[1 + slot : 2 + slot], axis=1, keepdims=True)
            line = jnp.where(spots == slot, value, line)
        slot_ref[...] = line
        copies.append(pltpu.make_async_copy(slot_ref, slot_out, sems.at[len(strips)]))
        copies[-1].start()
    else:
        means_out[...] = means
    for copy in copies:
        copy.wait()


def step(momentum, gradient, assignment):
    _, layers, rows, width = momentum.shape
    owners = lax.axis_size("dp")
    sections = lax.axis_size("section")
    chips = owners // 2
    tail = width - 2 * LANES
    assert chips == layers and chips & (chips - 1) == 0 and LANES % tail == 0 and 3 * layers <= LANES
    everyone = sections * owners
    entries = everyone * layers * rows * width
    mom = jnp.swapaxes(momentum[0], 1, 2)
    grad = jnp.swapaxes(gradient[0], 1, 2)
    anywhere = pl.BlockSpec(memory_space=pl.ANY)
    near_by = pl.BlockSpec(memory_space=pltpu.VMEM)
    sums, grad_near, mom_near = pl.pallas_call(
        functools.partial(sums_kernel, layers),
        in_specs=[anywhere, anywhere],
        out_specs=[near_by] * 3,
        out_shape=[
            jax.ShapeDtypeStruct((everyone, LANES), F32),
            jax.ShapeDtypeStruct(grad.shape, BF16),
            jax.ShapeDtypeStruct(mom.shape, F32),
        ],
        scratch_shapes=[
            pltpu.VMEM((-(-3 * layers // 8) * 8, rows), F32),
            pltpu.SemaphoreType.DMA((layers, 2)),
        ],
        compiler_params=params(),
        name="sums",
    )(pltpu.with_memory_space_constraint(grad, pltpu.HBM), pltpu.with_memory_space_constraint(mom, pltpu.HBM))
    sums = lax.all_to_all(sums, ("section", "dp"), 0, 0, tiled=True)

    packed = packed_rows(tail)
    half = packed // 2
    start, keep, send, factor = pl.pallas_call(
        functools.partial(start_kernel, layers, entries, owners),
        in_specs=[near_by] * 3,
        out_specs=[near_by] * 4,
        out_shape=[
            jax.ShapeDtypeStruct((layers, width, rows), BF16),
            jax.ShapeDtypeStruct((layers, half, LANES), F32),
            jax.ShapeDtypeStruct((layers, half, LANES), F32),
            jax.ShapeDtypeStruct((8, LANES), F32),
        ],
        scratch_shapes=[pltpu.VMEM((2, packed, LANES), F32)],
        compiler_params=params(),
        name="start",
    )(sums, grad_near, mom_near)

    def turn(value, by):
        return lax.ppermute(value, "dp", [(i, i ^ by) for i in range(owners)])

    chip_sums = keep + turn(send, 1)
    own = chip_sums[0]
    for rel in range(1, chips):
        own = own + turn(chip_sums[rel], 2 * rel)
    fresh = momentum_decay * mom_near + factor[0, 0] * grad_near.astype(F32)
    own, fresh = lax.optimization_barrier((own, fresh))
    other = turn(own, 1)

    full_rows = sent_rows(tail)
    piece = full_rows // 2
    mine, theirs = pl.pallas_call(
        functools.partial(newton_kernel, owners, width),
        in_specs=[near_by] * 2,
        out_specs=[near_by] * 2,
        out_shape=[jax.ShapeDtypeStruct((piece, LANES), BF16)] * 2,
        scratch_shapes=[
            pltpu.VMEM((packed, LANES), F32),
            pltpu.VMEM((packed, LANES), F32),
            pltpu.VMEM((full_rows, LANES), BF16),
        ],
        compiler_params=params(),
        name="newton",
    )(own, other)

    arriving = {}
    for k in range(1, chips):
        arriving[k] = turn(mine, 2 * k)
    update = means = None
    flops = 4 * width * width * rows
    for rel in range(chips):
        last = rel == chips - 1
        operands, in_specs = [start], [near_by] * 3
        aliases = {}
        if rel:
            near = arriving[rel]
            operands += [near, turn(near, 1)]
            operands += [means, update]
            in_specs += [near_by, pl.BlockSpec(memory_space=pl.ANY)]
            aliases = {4: 0}
        else:
            operands += [mine, theirs, assignment]
            in_specs.append(pl.BlockSpec(memory_space=pltpu.SMEM))
        call = pl.pallas_call(
            functools.partial(update_kernel, math.sqrt(owners * rows), width, rel, last),
            in_specs=in_specs,
            out_specs=[
                pl.BlockSpec(memory_space=pl.ANY),
                pl.BlockSpec(memory_space=pl.ANY) if last else near_by,
            ],
            out_shape=[
                jax.ShapeDtypeStruct((layers, width, rows), BF16),
                jax.ShapeDtypeStruct((1, MAXOWN) if last else (8, LANES), F32),
            ],
            scratch_shapes=[
                pltpu.VMEM((full_rows, LANES), BF16),
                pltpu.VMEM((width, rows), BF16),
                pltpu.SemaphoreType.DMA((4,)),
            ]
            + [pltpu.VMEM((1, MAXOWN), F32)] * last,
            input_output_aliases=aliases,
            compiler_params=params(),
            cost_estimate=cost(flops, 4 * width * rows + 4 * piece * LANES),
            name="update",
        )
        update, means = call(*operands)
    return (jnp.swapaxes(fresh, 1, 2)[None], jnp.swapaxes(update, 1, 2)[None], means)


def solution(mesh):
    in_specs = (P("section", None, "dp", None), P("section", None, "dp", None), P("section", None))
    out_specs = (P("section", None, "dp", None), P("section", None, "dp", None), P("section", "dp"))
    return jax.shard_map(step, mesh=mesh, in_specs=in_specs, out_specs=out_specs, check_vma=False)
```
